32 devices in a mesh: shard: 4 (over x, core), rep: 8 (over z, y).
Axes of the slice: x: 2, y: 2, z: 4, core: 2. Of those that a mesh axis runs over, the one named last changes fastest.
Arguments:
- tokens: bfloat16 [8, 512, 1024], P('rep', 'shard'), may hold values from -6 to 6
- cotangent: bfloat16 [8, 512, 1024], P('rep', 'shard'), may hold values from -6 to 6
- segment_ids: int32 [8, 512], P('rep'), may hold values from 0 to 3, never falling along the last dimension, each value on 1 to 256 neighbouring positions
- intake: float32 [3, 1024, 1024], P(None, ('shard', 'rep')), may hold values from -0.1875 to 0.1875
- outlet: float32 [1024, 1024], P(('shard', 'rep')), may hold values from -1.5 to 1.5
- expand: float32 [4096, 1024], P(('shard', 'rep')), may hold values from -0.1875 to 0.1875
- shrink: float32 [4096, 1024], P(('shard', 'rep')), may hold values from -0.09375 to 0.09375
- affine: float32 [8, 1024], P(None, ('shard', 'rep')), may hold values from -0.8 to 0.8
- offset: float32 [4096], P(('shard', 'rep')), may hold values from -0.8 to 0.8
- intake_first: float32 [3, 1024, 1024], P(None, ('shard', 'rep')), may hold values from -15 to 15
- outlet_first: float32 [1024, 1024], P(('shard', 'rep')), may hold values from -15 to 15
- expand_first: float32 [4096, 1024], P(('shard', 'rep')), may hold values from -15 to 15
- shrink_first: float32 [4096, 1024], P(('shard', 'rep')), may hold values from -15 to 15
- affine_first: float32 [8, 1024], P(None, ('shard', 'rep')), may hold values from -15 to 15
- offset_first: float32 [4096], P(('shard', 'rep')), may hold values from -15 to 15
- intake_second: float32 [3, 1024, 1024], P(None, ('shard', 'rep')), may hold values from 1 to 100
- outlet_second: float32 [1024, 1024], P(('shard', 'rep')), may hold values from 1 to 100
- expand_second: float32 [4096, 1024], P(('shard', 'rep')), may hold values from 1 to 100
- shrink_second: float32 [4096, 1024], P(('shard', 'rep')), may hold values from 1 to 100
- affine_second: float32 [8, 1024], P(None, ('shard', 'rep')), may hold values from 1 to 100
- offset_second: float32 [4096], P(('shard', 'rep')), may hold values from 1 to 100
Outputs:
- layer_out: bfloat16 [8, 512, 1024], P('rep', 'shard')
- token_grad: bfloat16 [8, 512, 1024], P('rep', 'shard')
- intake_grad: float32 [3, 1024, 1024], P(None, ('shard', 'rep'))
- outlet_grad: float32 [1024, 1024], P(('shard', 'rep'))
- expand_grad: float32 [4096, 1024], P(('shard', 'rep'))
- shrink_grad: float32 [4096, 1024], P(('shard', 'rep'))
- affine_grad: float32 [8, 1024], P(None, ('shard', 'rep'))
- offset_grad: float32 [4096], P(('shard', 'rep'))
- intake_next: float32 [3, 1024, 1024], P(None, ('shard', 'rep'))
- outlet_next: float32 [1024, 1024], P(('shard', 'rep'))
- expand_next: float32 [4096, 1024], P(('shard', 'rep'))
- shrink_next: float32 [4096, 1024], P(('shard', 'rep'))
- affine_next: float32 [8, 1024], P(None, ('shard', 'rep'))
- offset_next: float32 [4096], P(('shard', 'rep'))
- intake_momentum: float32 [3, 1024, 1024], P(None, ('shard', 'rep'))
- outlet_momentum: float32 [1024, 1024], P(('shard', 'rep'))
- expand_momentum: float32 [4096, 1024], P(('shard', 'rep'))
- shrink_momentum: float32 [4096, 1024], P(('shard', 'rep'))
- affine_momentum: float32 [8, 1024], P(None, ('shard', 'rep'))
- offset_momentum: float32 [4096], P(('shard', 'rep'))
- intake_variance: float32 [3, 1024, 1024], P(None, ('shard', 'rep'))
- outlet_variance: float32 [1024, 1024], P(('shard', 'rep'))
- expand_variance: float32 [4096, 1024], P(('shard', 'rep'))
- shrink_variance: float32 [4096, 1024], P(('shard', 'rep'))
- affine_variance: float32 [8, 1024], P(None, ('shard', 'rep'))
- offset_variance: float32 [4096], P(('shard', 'rep'))
The draws below stay inside these ranges and needn't reach their ends.
Inputs may be any that keep to these rules, and one draw needn't show every extreme that they name: `segment_ids`: within each sequence the numbers never fall along positions, every number appears, each document spans at most 256 positions and one spans exactly that many.
All inputs are finite; a program needn't handle non-finite values.
Results may differ from the reference program's by a relative error of at most 0.025.
Values may be sent and summed in bfloat16 or wider, within the bound.
No kernel may reach another device: no remote copies, remote signals or barrier semaphores. Data moves between devices by JAX's collectives and lax.ppermute only.
A program may use at most 128 MiB of HBM per device.

```python
import math
import jax
import jax.numpy as jnp
import numpy as np
from jax import lax

D = 1024
HEADS = 16
HEAD_DIM = 64
FF = 4096
LEN = 512
DOCS = 4
SEQS = 8


def block_levels(rng, shape, shards, low, top_value):
    def one(dim, blocks):
        steps = jax.random.uniform(jax.random.fold_in(jax.random.fold_in(rng, 6), dim), (blocks,), jnp.float32, low / len(shards), top_value / len(shards))
        return jnp.repeat(jnp.exp(steps), shape[dim] // blocks).reshape((-1,) + (1,) * (len(shape) - dim - 1))

    level = one(*shards[0])
    for cut in shards[1:]:
        level = level * one(*cut)
    return level


def profile(amount, total, bound, lean):
    portions = [(1 << 20) // math.isqrt(standing ** lean) + 1 for standing in range(2, amount + 1)]
    surplus, holding = total - bound - (amount - 1), [1] * (amount - 1)
    while surplus > 0:
        candidates = [i for i in range(amount - 1) if holding[i] < bound]
        whole, remaining = sum([portions[i] for i in candidates]), surplus
        for i in candidates:
            extra = min(bound - holding[i], max(1, remaining * portions[i] // whole), surplus)
            holding[i] = holding[i] + extra
            surplus = surplus - extra
    return np.array([bound] + holding)


def uneven_parts(own_key, count, total, most, slope):
    if count == 2:
        one = jax.random.randint(own_key, (), max(1, total - most), min(most, total - 1) + 1)
        return jnp.stack([one, total - one])
    tallies = jnp.asarray(profile(count, total, most, slope), jnp.int32)
    twos = (count - 1) // 2
    source_of, taker = tallies[1:1 + 2 * twos:2], tallies[2:2 + 2 * twos:2]
    margin = jnp.minimum(source_of - 1, most - taker)
    passed = jax.random.randint(jax.random.fold_in(own_key, 1), (twos,), 0, 1 << 20) % (margin + 1)
    tallies = tallies.at[1:1 + 2 * twos:2].set(source_of - passed).at[2:2 + 2 * twos:2].set(taker + passed)
    return tallies[jax.random.permutation(jax.random.fold_in(own_key, 2), count)]


def bell_draw(own_key, shape, scale, reach, shards=(), held_as=jnp.bfloat16):
    drawn = scale * jax.random.normal(own_key, shape, jnp.float32)
    if shards:
        drawn = drawn * block_levels(own_key, shape, shards, -0.22, 0.18)
    return jnp.clip(drawn, -reach, reach).astype(held_as)


def setup_inputs(seed: int = 0) -> dict:
    seeds = jax.random.split(jax.random.key(seed), 22)
    tokens = bell_draw(seeds[0], (SEQS, LEN, D), 1.0, 6.0, ((0, 8), (1, 4)))
    cotangent = bell_draw(seeds[1], (SEQS, LEN, D), 1.0, 6.0, ((0, 8), (1, 4)))
    segment_ids = jax.vmap(lambda own: jnp.searchsorted(jnp.cumsum(uneven_parts(own, DOCS, LEN, LEN // 2, 0)), jnp.arange(LEN), side="right"))(jax.random.split(seeds[2], SEQS)).reshape((SEQS, LEN)).astype(jnp.int32)
    intake = bell_draw(seeds[3], (3, D, D), D ** -0.5, 0.1875, ((1, 32),), jnp.float32)
    outlet = bell_draw(seeds[4], (D, D), (D // 64) ** -0.5, 1.5, ((0, 32),), jnp.float32)
    expand = bell_draw(seeds[5], (FF, D), D ** -0.5, 0.1875, ((0, 32),), jnp.float32)
    shrink = bell_draw(seeds[6], (FF, D), FF ** -0.5, 0.09375, ((0, 32),), jnp.float32)
    affine = bell_draw(seeds[7], (8, D), 0.2, 0.8, ((1, 32),), jnp.float32)
    offset = bell_draw(seeds[8], (FF,), 0.2, 0.8, ((0, 32),), jnp.float32)
    intake_first = bell_draw(seeds[9], (3, D, D), 3.0, 15.0, ((1, 32),), jnp.float32)
    outlet_first = bell_draw(seeds[10], (D, D), 3.0, 15.0, ((0, 32),), jnp.float32)
    expand_first = bell_draw(seeds[11], (FF, D), 3.0, 15.0, ((0, 32),), jnp.float32)
    shrink_first = bell_draw(seeds[12], (FF, D), 3.0, 15.0, ((0, 32),), jnp.float32)
    affine_first = bell_draw(seeds[13], (8, D), 3.0, 15.0, ((1, 32),), jnp.float32)
    offset_first = bell_draw(seeds[14], (FF,), 3.0, 15.0, ((0, 32),), jnp.float32)
    intake_second = jnp.clip(jnp.exp(math.log(100.0) - 4.6051702 * jax.random.uniform(seeds[15], (3, D, D), jnp.float32) ** block_levels(seeds[15], (3, D, D), ((1, 32),), -0.2, 0.2)), 1.0, 100.0)
    outlet_second = jnp.clip(jnp.exp(math.log(100.0) - 4.6051702 * jax.random.uniform(seeds[16], (D, D), jnp.float32) ** block_levels(seeds[16], (D, D), ((0, 32),), -0.2, 0.2)), 1.0, 100.0)
    expand_second = jnp.clip(jnp.exp(math.log(100.0) - 4.6051702 * jax.random.uniform(seeds[17], (FF, D), jnp.float32) ** block_levels(seeds[17], (FF, D), ((0, 32),), -0.2, 0.2)), 1.0, 100.0)
    shrink_second = jnp.clip(jnp.exp(math.log(100.0) - 4.6051702 * jax.random.uniform(seeds[18], (FF, D), jnp.float32) ** block_levels(seeds[18], (FF, D), ((0, 32),), -0.2, 0.2)), 1.0, 100.0)
    affine_second = jnp.clip(jnp.exp(math.log(100.0) - 4.6051702 * jax.random.uniform(seeds[19], (8, D), jnp.float32) ** block_levels(seeds[19], (8, D), ((1, 32),), -0.2, 0.2)), 1.0, 100.0)
    offset_second = jnp.clip(jnp.exp(math.log(100.0) - 4.6051702 * jax.random.uniform(seeds[20], (FF,), jnp.float32) ** block_levels(seeds[20], (FF,), ((0, 32),), -0.2, 0.2)), 1.0, 100.0)
    return {"tokens": tokens, "cotangent": cotangent, "segment_ids": segment_ids, "intake": intake, "outlet": outlet, "expand": expand, "shrink": shrink, "affine": affine, "offset": offset, "intake_first": intake_first, "outlet_first": outlet_first, "expand_first": expand_first, "shrink_first": shrink_first, "affine_first": affine_first, "offset_first": offset_first, "intake_second": intake_second, "outlet_second": outlet_second, "expand_second": expand_second, "shrink_second": shrink_second, "affine_second": affine_second, "offset_second": offset_second}


lr_rate = 0.03
beta_one = 0.9
beta_two = 0.95
adam_eps = 1e-08
weight_decay = 0.1
step_count = 3
norm_eps = 1e-05

def layer_norm(values_in):
    centred = values_in - lax.optimization_barrier(jnp.mean(values_in, axis=-1, keepdims=True))
    inv_std = lax.rsqrt(lax.optimization_barrier(jnp.mean(centred * centred, axis=-1, keepdims=True)) + norm_eps)
    return (centred * inv_std, inv_std)

def norm_back(grad_normed, normed, inv_std):
    return inv_std * (grad_normed - lax.optimization_barrier(jnp.mean(grad_normed, axis=-1, keepdims=True)) - normed * lax.optimization_barrier(jnp.mean(grad_normed * normed, axis=-1, keepdims=True)))

def gelu_value(hidden):
    return 0.5 * hidden * (1.0 + jax.scipy.special.erf(hidden / math.sqrt(2.0)))

def gelu_slope(hidden):
    return 0.5 * (1.0 + jax.scipy.special.erf(hidden / math.sqrt(2.0))) + hidden * jnp.exp(-0.5 * hidden * hidden) / math.sqrt(2.0 * math.pi)

def adamw_step(weight, first_mom, second_mom, gradient):
    momentum = beta_one * first_mom + (1.0 - beta_one) * gradient
    variance = beta_two * second_mom + (1.0 - beta_two) * gradient * gradient
    fixed_mom = momentum / (1.0 - beta_one ** step_count)
    fixed_var = variance / (1.0 - beta_two ** step_count)
    return (weight - lr_rate * (fixed_mom / (jnp.sqrt(fixed_var) + adam_eps) + weight_decay * weight), momentum, variance)

def plain_dot(left_side, right_side):
    return jnp.dot(left_side, right_side, preferred_element_type=jnp.float32)

def reference(tokens, cotangent, segment_ids, intake, outlet, expand, shrink, affine, offset, intake_first, outlet_first, expand_first, shrink_first, affine_first, offset_first, intake_second, outlet_second, expand_second, shrink_second, affine_second, offset_second):
    half_intake = intake.astype(jnp.bfloat16).reshape(3 * D, D)
    half_outlet = outlet.astype(jnp.bfloat16)
    half_expand = expand.astype(jnp.bfloat16)
    half_shrink = shrink.astype(jnp.bfloat16)
    coeffs = lax.optimization_barrier(affine.astype(jnp.bfloat16)).astype(jnp.float32)
    unit_bias = lax.optimization_barrier(offset.astype(jnp.bfloat16)).astype(jnp.float32)
    score_scale = 1.0 / math.sqrt(HEAD_DIM)

    def one_sequence(carried, inputs):
        source, cot_rows, seg_rows = inputs
        same_doc = (seg_rows[:, None] == seg_rows[None, :])[None]
        qkv_rows = plain_dot(source, half_intake.T)
        query_half = (qkv_rows[:, :D] + coeffs[0]).astype(jnp.bfloat16)
        key_half = qkv_rows[:, D:2 * D].astype(jnp.bfloat16)
        value_half = (qkv_rows[:, 2 * D:] + coeffs[1]).astype(jnp.bfloat16)
        query_heads = query_half.reshape(LEN, HEADS, HEAD_DIM).astype(jnp.float32)
        key_heads = key_half.reshape(LEN, HEADS, HEAD_DIM).astype(jnp.float32)
        value_heads = value_half.reshape(LEN, HEADS, HEAD_DIM).astype(jnp.float32)
        scores = jnp.einsum('qhd,khd->hqk', query_heads, key_heads) * score_scale
        exp_scores = jnp.where(same_doc, jnp.exp(scores), 0.0)
        totals = lax.optimization_barrier(jnp.sum(exp_scores, axis=-1, keepdims=True))
        log_total = jnp.log(totals)
        prob_half = (exp_scores / totals).astype(jnp.bfloat16)
        attended = jnp.einsum('hqk,khd->qhd', prob_half.astype(jnp.float32), value_heads).reshape(LEN, D).astype(jnp.bfloat16)
        resid_one = source.astype(jnp.float32) + plain_dot(attended, half_outlet) + coeffs[2]
        normed_one, inv_one = layer_norm(resid_one)
        mixed_one = normed_one * (1.0 + coeffs[3]) + coeffs[4]
        inner_in = mixed_one.astype(jnp.bfloat16)
        hidden = plain_dot(inner_in, half_expand.T) + unit_bias
        act_half = gelu_value(hidden).astype(jnp.bfloat16)
        resid_two = mixed_one + plain_dot(act_half, half_shrink) + coeffs[5]
        normed_two, inv_two = layer_norm(resid_two)
        out_rows = (normed_two * (1.0 + coeffs[6]) + coeffs[7]).astype(jnp.bfloat16)
        out_grad = cot_rows.astype(jnp.float32)
        gain_two = lax.optimization_barrier(jnp.sum(out_grad * normed_two, axis=0))
        shift_two = lax.optimization_barrier(jnp.sum(out_grad, axis=0))
        grad_two = norm_back(out_grad * (1.0 + coeffs[6]), normed_two, inv_two)
        bias_two = lax.optimization_barrier(jnp.sum(grad_two, axis=0))
        grad_half = grad_two.astype(jnp.bfloat16)
        shrink_term = plain_dot(act_half.T, grad_half)
        grad_hidden = plain_dot(grad_half, half_shrink.T) * gelu_slope(hidden)
        offset_term = lax.optimization_barrier(jnp.sum(grad_hidden, axis=0))
        hidden_half = grad_hidden.astype(jnp.bfloat16)
        expand_term = plain_dot(hidden_half.T, inner_in)
        grad_mixed = grad_two + plain_dot(hidden_half, half_expand)
        gain_one = lax.optimization_barrier(jnp.sum(grad_mixed * normed_one, axis=0))
        shift_one = lax.optimization_barrier(jnp.sum(grad_mixed, axis=0))
        grad_one = norm_back(grad_mixed * (1.0 + coeffs[3]), normed_one, inv_one)
        bias_out = lax.optimization_barrier(jnp.sum(grad_one, axis=0))
        one_half = grad_one.astype(jnp.bfloat16)
        outlet_term = plain_dot(attended.T, one_half)
        attend_grad = plain_dot(one_half, half_outlet.T).astype(jnp.bfloat16)
        grad_heads = attend_grad.reshape(LEN, HEADS, HEAD_DIM).astype(jnp.float32)
        scores_again = jnp.einsum('qhd,khd->hqk', query_heads, key_heads) * score_scale
        prob_again = jnp.where(same_doc, jnp.exp(scores_again - log_total), 0.0)
        prob_grad = jnp.einsum('qhd,khd->hqk', grad_heads, value_heads)
        row_dots = lax.optimization_barrier(jnp.sum(prob_again * prob_grad, axis=-1, keepdims=True))
        score_half = (prob_again * (prob_grad - row_dots)).astype(jnp.bfloat16).astype(jnp.float32)
        query_grad = (jnp.einsum('hqk,khd->qhd', score_half, key_heads) * score_scale).reshape(LEN, D)
        key_grad = (jnp.einsum('hqk,qhd->khd', score_half, query_heads) * score_scale).reshape(LEN, D)
        value_grad = jnp.einsum('hqk,qhd->khd', prob_again.astype(jnp.bfloat16).astype(jnp.float32), grad_heads).reshape(LEN, D)
        qkv_half = jnp.concatenate([query_grad, key_grad, value_grad], axis=1).astype(jnp.bfloat16)
        intake_term = plain_dot(qkv_half.T, source).reshape(3, D, D)
        input_rows = (grad_one + plain_dot(qkv_half, half_intake)).astype(jnp.bfloat16)
        affine_term = jnp.stack([lax.optimization_barrier(jnp.sum(query_grad, axis=0)), lax.optimization_barrier(jnp.sum(value_grad, axis=0)), bias_out, gain_one, shift_one, bias_two, gain_two, shift_two])
        terms = (intake_term, outlet_term, expand_term, shrink_term, affine_term, offset_term)
        carried = tuple((total_now + term_now for total_now, term_now in zip(carried, terms)))
        return (carried, (out_rows, input_rows))
    start_sums = (jnp.zeros(intake.shape, jnp.float32), jnp.zeros(outlet.shape, jnp.float32), jnp.zeros(expand.shape, jnp.float32), jnp.zeros(shrink.shape, jnp.float32), jnp.zeros(affine.shape, jnp.float32), jnp.zeros(offset.shape, jnp.float32))
    grad_sums, (layer_out, token_grad) = lax.scan(one_sequence, start_sums, (tokens, cotangent, segment_ids))
    intake_grad, outlet_grad, expand_grad, shrink_grad, affine_grad, offset_grad = grad_sums
    intake_next, intake_momentum, intake_variance = adamw_step(intake, intake_first, intake_second, intake_grad)
    outlet_next, outlet_momentum, outlet_variance = adamw_step(outlet, outlet_first, outlet_second, outlet_grad)
    expand_next, expand_momentum, expand_variance = adamw_step(expand, expand_first, expand_second, expand_grad)
    shrink_next, shrink_momentum, shrink_variance = adamw_step(shrink, shrink_first, shrink_second, shrink_grad)
    affine_next, affine_momentum, affine_variance = adamw_step(affine, affine_first, affine_second, affine_grad)
    offset_next, offset_momentum, offset_variance = adamw_step(offset, offset_first, offset_second, offset_grad)
    return (layer_out, token_grad, intake_grad, outlet_grad, expand_grad, shrink_grad, affine_grad, offset_grad, intake_next, outlet_next, expand_next, shrink_next, affine_next, offset_next, intake_momentum, outlet_momentum, expand_momentum, shrink_momentum, affine_momentum, offset_momentum, intake_variance, outlet_variance, expand_variance, shrink_variance, affine_variance, offset_variance)
```

```python
import itertools
import math

import jax
import jax.numpy as jnp
from jax import lax
from jax.experimental import pallas as pl
from jax.experimental.pallas import tpu as pltpu
from jax.sharding import PartitionSpec as P

HEAD_DIM = 64


lr_rate = 0.03
beta_one = 0.9
beta_two = 0.95
adam_eps = 1e-08
weight_decay = 0.1
step_count = 3
norm_eps = 1e-05

f32 = jnp.float32
bf16 = jnp.bfloat16


def layer_norm(values_in):
    centred = values_in - jnp.mean(values_in, axis=-1, keepdims=True)
    inv_std = lax.rsqrt(jnp.mean(centred * centred, axis=-1, keepdims=True) + norm_eps)
    return (centred * inv_std, inv_std)


def norm_back(grad_normed, normed, inv_std):
    return inv_std * (
        grad_normed
        - jnp.mean(grad_normed, axis=-1, keepdims=True)
        - normed * jnp.mean(grad_normed * normed, axis=-1, keepdims=True)
    )


def gelu_value(hidden):
    return 0.5 * hidden * (1.0 + jax.scipy.special.erf(hidden / math.sqrt(2.0)))


def gelu_slope(hidden):
    return 0.5 * (1.0 + jax.scipy.special.erf(hidden / math.sqrt(2.0))) + hidden * jnp.exp(
        -0.5 * hidden * hidden
    ) / math.sqrt(2.0 * math.pi)


def adamw_step(weight, first_mom, second_mom, gradient):
    momentum = beta_one * first_mom + (1.0 - beta_one) * gradient
    variance = beta_two * second_mom + (1.0 - beta_two) * gradient * gradient
    fixed_mom = momentum / (1.0 - beta_one**step_count)
    fixed_var = variance / (1.0 - beta_two**step_count)
    return (
        weight - lr_rate * (fixed_mom / (jnp.sqrt(fixed_var) + adam_eps) + weight_decay * weight),
        momentum,
        variance,
    )


def dot_on(left_side, right_side, left_dim, right_dim):
    return lax.dot_general(
        left_side,
        right_side,
        (((left_dim,), (right_dim,)), ((), ())),
        preferred_element_type=f32,
    )


def dot_plain(left_side, right_side):
    return dot_on(left_side, right_side, 1, 0)


def dot_rows(left_side, right_side):
    return dot_on(left_side, right_side, 1, 1)


def dot_cols(left_side, right_side):
    return dot_on(left_side, right_side, 0, 0)


def masked_exp(query_head, key_head, same_doc):
    scores = dot_cols(key_head, query_head) * (1.0 / math.sqrt(HEAD_DIM))
    exp_scores = jnp.where(same_doc, jnp.exp(scores), 0.0)
    return exp_scores / jnp.sum(exp_scores, axis=0, keepdims=True)


def attend_kernel(query_ref, key_ref, value_ref, seg_col_ref, seg_row_ref, out_ref):
    same_doc = seg_col_ref[...] == seg_row_ref[...]
    for start in range(0, query_ref.shape[0], HEAD_DIM):
        rows = slice(start, start + HEAD_DIM)
        probs = masked_exp(query_ref[rows, :], key_ref[rows, :], same_doc)
        out_ref[rows, :] = dot_plain(value_ref[rows, :], probs.astype(bf16)).astype(bf16)


def attend_back_kernel(
    query_ref, key_ref, value_ref, grad_ref, seg_col_ref, seg_row_ref, dq_ref, dk_ref, dv_ref, sum_ref
):
    score_scale = 1.0 / math.sqrt(HEAD_DIM)
    same_doc = seg_col_ref[...] == seg_row_ref[...]
    for start in range(0, query_ref.shape[0], HEAD_DIM):
        rows = slice(start, start + HEAD_DIM)
        query_head = query_ref[rows, :]
        key_head = key_ref[rows, :]
        grad_head = grad_ref[rows, :]
        probs = masked_exp(query_head, key_head, same_doc)
        prob_grad = dot_cols(value_ref[rows, :], grad_head)
        row_dots = jnp.sum(probs * prob_grad, axis=0, keepdims=True)
        score_half = (probs * (prob_grad - row_dots)).astype(bf16)
        dq = dot_plain(key_head, score_half) * score_scale
        dv = dot_rows(grad_head, probs.astype(bf16))
        dq_ref[rows, :] = dq.astype(bf16)
        dk_ref[rows, :] = (dot_rows(query_head, score_half) * score_scale).astype(bf16)
        dv_ref[rows, :] = dv.astype(bf16)
        sum_ref[rows, 0:1] = jnp.sum(dq, axis=1, keepdims=True)
        sum_ref[rows, 1:2] = jnp.sum(dv, axis=1, keepdims=True)


def factor_rep(count, first):
    factors = [first]
    count //= first
    while count > 1:
        step = 4 if count % 4 == 0 else 2
        factors.append(step)
        count //= step
    return factors


def make_body(groups, replicas):
    shard_bits = [1 << i for i in range(groups.bit_length() - 1)]
    rep_bits = [1 << i for i in range(replicas.bit_length() - 1)]

    def swap(value, axis, count, bit):
        return lax.ppermute(value, axis, [(i, i ^ bit) for i in range(count)])

    def gather_group(piece):
        pieces = {0: piece}
        for bit in reversed(shard_bits):
            for slot in list(pieces):
                pieces[slot ^ bit] = swap(pieces[slot], "shard", groups, bit)
        return [pieces[i] for i in range(groups)]

    def scatter_group(pieces):
        pieces = dict(enumerate(pieces))
        for bit in shard_bits:
            for slot in sorted((s for s in pieces if s & bit), reverse=True):
                sent = pieces.pop(slot).astype(bf16)
                pieces[slot ^ bit] = pieces[slot ^ bit] + swap(sent, "shard", groups, bit).astype(f32)
        return pieces[0]

    def sum_all(value):
        for bit in shard_bits:
            value = value + swap(value, "shard", groups, bit)
        for bit in rep_bits:
            value = value + swap(value, "rep", replicas, bit)
        return value

    def body(
        tokens,
        cotangent,
        segment_ids,
        intake,
        outlet,
        expand,
        shrink,
        affine,
        offset,
        intake_first,
        outlet_first,
        expand_first,
        shrink_first,
        affine_first,
        offset_first,
        intake_second,
        outlet_second,
        expand_second,
        shrink_second,
        affine_second,
        offset_second,
    ):
        own_rows = tokens.shape[1]
        width = tokens.shape[2]
        seq_len = own_rows * groups
        head_cols = intake.shape[1] * replicas
        factors = factor_rep(replicas, head_cols // HEAD_DIM)
        strides = [math.prod(factors[i + 1 :]) for i in range(len(factors))]
        lead = factors[0]
        suffixes = list(itertools.product(*[range(f) for f in factors[1:]]))
        own_shard = lax.axis_index("shard")
        own_rep = lax.axis_index("rep")

        def shift(value, level, amount):
            pairs = []
            for r in range(replicas):
                coord = (r // strides[level]) % factors[level]
                moved = (coord + amount) % factors[level]
                pairs.append((r, r + (moved - coord) * strides[level]))
            return lax.ppermute(value, "rep", pairs)

        def gather_rep(piece):
            lead_parts = [piece] + [shift(piece, 0, k) for k in range(1, lead)]
            if len(factors) > 2:
                return gather_rest({(): jnp.concatenate(lead_parts, axis=0)})
            blocks = [lead_parts]
            for k in range(1, len(suffixes)):
                blocks.append([shift(v, 1, k) for v in lead_parts])
            return [jnp.concatenate(parts, axis=0) for parts in blocks]

        def gather_rest(blocks):
            for level in range(1, len(factors)):
                joined = jnp.concatenate(list(blocks.values()), axis=0)
                grown = {s + (0,): v for s, v in blocks.items()}
                for k in range(1, factors[level]):
                    came = jnp.split(shift(joined, level, k), len(blocks))
                    grown.update({s + (k,): v for s, v in zip(blocks, came)})
                blocks = grown
            return [blocks[s] for s in suffixes]

        def interleave(blocks):
            rows = blocks[0].shape[0] // lead
            stacked = jnp.stack([b.reshape(lead, rows, -1) for b in blocks], axis=1)
            return stacked.reshape(lead * len(blocks) * rows, -1)

        def separate(value):
            rows = value.shape[0] // replicas
            split = value.reshape(lead, len(suffixes), rows, -1)
            return [split[:, i].reshape(lead * rows, -1) for i in range(len(suffixes))]

        def scatter_rep(blocks, wire=bf16):
            blocks = dict(zip(suffixes, blocks))
            for level in reversed(range(1, len(factors))):
                merged = {s[:-1]: v for s, v in blocks.items() if s[-1] == 0}
                for k in range(1, factors[level]):
                    joined = [blocks[s + (k,)].astype(wire) for s in merged]
                    came = shift(jnp.concatenate(joined, axis=0), level, -k)
                    for s, v in zip(list(merged), jnp.split(came, len(merged))):
                        merged[s] = merged[s] + v.astype(f32)
                blocks = merged
            whole = blocks[()]
            rows = whole.shape[0] // lead
            total = whole[:rows]
            for k in range(1, lead):
                came = shift(whole[k * rows : (k + 1) * rows].astype(wire), 0, -k)
                total = total + came.astype(f32)
            return total

        own_cols = affine.shape[1]
        placed = lax.dynamic_update_slice(
            jnp.zeros((affine.shape[0], width), bf16),
            affine.astype(bf16),
            (0, (own_shard * replicas + own_rep) * own_cols),
        )
        coeffs = sum_all(placed).astype(f32)

        source = tokens.reshape(own_rows, width)
        group_tokens = jnp.concatenate(gather_group(source), axis=0)
        intake_low = intake.astype(bf16)
        w_query, w_key, w_value = [interleave(gather_rep(intake_low[i])) for i in range(3)]
        w_out = interleave(gather_rep(outlet.astype(bf16)))
        unit_bias = gather_rep(offset.astype(bf16).reshape(1, -1))
        unit_bias = [b.reshape(1, -1).astype(f32) for b in unit_bias]
        w_expand = gather_rep(expand.astype(bf16))
        w_shrink = gather_rep(shrink.astype(bf16))

        column = lax.broadcasted_iota(jnp.int32, (head_cols, 1), 0)
        block = column // own_cols
        feature_rep = jnp.zeros_like(block)
        for stride, factor in zip(strides, factors):
            slot = (block // stride) % factor
            coord = (own_rep // stride) % factor
            feature_rep = feature_rep + ((coord - slot + factor) % factor) * stride
        feature = (own_shard * replicas + feature_rep) * own_cols + column % own_cols
        picks = feature == lax.broadcasted_iota(jnp.int32, (head_cols, width), 1)
        head_bias = dot_rows(picks.astype(bf16), coeffs[0:2].astype(bf16))

        every_seg = segment_ids.reshape(seq_len)
        seg_slots = jnp.concatenate(
            [
                lax.dynamic_slice_in_dim(every_seg, (own_shard ^ k) * own_rows, own_rows)
                for k in range(groups)
            ]
        )
        seg_col = seg_slots.reshape(seq_len, 1)
        seg_row = seg_slots.reshape(1, seq_len)

        query = (dot_rows(w_query, group_tokens) + head_bias[:, 0:1]).astype(bf16)
        key = dot_rows(w_key, group_tokens).astype(bf16)
        value = (dot_rows(w_value, group_tokens) + head_bias[:, 1:2]).astype(bf16)
        like_heads = jax.ShapeDtypeStruct((head_cols, seq_len), bf16)
        attended = pl.pallas_call(attend_kernel, out_shape=like_heads, name="attend")(
            query, key, value, seg_col, seg_row
        )

        def token_slots(product):
            return [product[i * own_rows : (i + 1) * own_rows] for i in range(groups)]

        attn_out = scatter_group(token_slots(dot_cols(attended, w_out)))
        resid_one = source.astype(f32) + attn_out + coeffs[2]
        normed_one, inv_one = layer_norm(resid_one)
        mixed_one = normed_one * (1.0 + coeffs[3]) + coeffs[4]
        inner_in = mixed_one.astype(bf16)
        group_in = jnp.concatenate(gather_group(inner_in), axis=0)
        hidden = [dot_rows(group_in, w) + b for w, b in zip(w_expand, unit_bias)]
        act_half = [gelu_value(h).astype(bf16) for h in hidden]
        ffn_part = sum(dot_plain(a, w) for a, w in zip(act_half, w_shrink))
        ffn_out = scatter_group(token_slots(ffn_part))
        resid_two = mixed_one + ffn_out + coeffs[5]
        normed_two, inv_two = layer_norm(resid_two)
        layer_out = (normed_two * (1.0 + coeffs[6]) + coeffs[7]).astype(bf16)

        out_grad = cotangent.reshape(own_rows, width).astype(f32)
        grad_two = norm_back(out_grad * (1.0 + coeffs[6]), normed_two, inv_two)
        group_grad = jnp.concatenate(gather_group(grad_two.astype(bf16)), axis=0)
        gain_two = jnp.sum(out_grad * normed_two, axis=0)
        shift_two = jnp.sum(out_grad, axis=0)
        bias_two = jnp.sum(grad_two, axis=0)
        grad_hidden = [
            dot_rows(group_grad, w) * gelu_slope(h) for w, h in zip(w_shrink, hidden)
        ]
        hidden_half = [g.astype(bf16) for g in grad_hidden]
        inner_part = sum(dot_plain(g, w) for g, w in zip(hidden_half, w_expand))
        shrink_grad = scatter_rep([dot_cols(a, group_grad) for a in act_half])
        grad_inner = scatter_group(token_slots(inner_part))
        expand_grad = scatter_rep([dot_cols(g, group_in) for g in hidden_half])
        offset_grad = scatter_rep(
            [jnp.sum(g, axis=0).reshape(lead, -1) for g in grad_hidden], f32
        ).reshape(offset.shape)
        grad_mixed = grad_two + grad_inner
        grad_one = norm_back(grad_mixed * (1.0 + coeffs[3]), normed_one, inv_one)
        gain_one = jnp.sum(grad_mixed * normed_one, axis=0)
        shift_one = jnp.sum(grad_mixed, axis=0)
        bias_out = jnp.sum(grad_one, axis=0)
        group_one = jnp.concatenate(gather_group(grad_one.astype(bf16)), axis=0)
        attend_grad = dot_rows(w_out, group_one).astype(bf16)
        outlet_grad = scatter_rep(separate(dot_plain(attended, group_one)))
        dq, dk, dv, head_sums = pl.pallas_call(
            attend_back_kernel,
            out_shape=(like_heads, like_heads, like_heads, jax.ShapeDtypeStruct((head_cols, 2), f32)),
            name="attend_back",
        )(query, key, value, attend_grad, seg_col, seg_row)
        intake_grad = jnp.stack(
            [scatter_rep(separate(dot_plain(g, group_tokens))) for g in (dq, dk, dv)]
        )
        input_part = dot_cols(dq, w_query) + dot_cols(dk, w_key) + dot_cols(dv, w_value)
        token_grad = (grad_one + scatter_group(token_slots(input_part))).astype(bf16)
        head_rows = lax.dot_general(
            head_sums,
            picks.astype(f32),
            (((0,), (0,)), ((), ())),
            precision=lax.Precision.HIGHEST,
            preferred_element_type=f32,
        )
        affine_rows = jnp.stack([bias_out, gain_one, shift_one, bias_two, gain_two, shift_two])
        affine_full = sum_all(jnp.concatenate([head_rows, affine_rows], axis=0))
        affine_grad = lax.dynamic_slice(
            affine_full, (0, (own_shard * replicas + own_rep) * own_cols), affine.shape
        )

        intake_next, intake_momentum, intake_variance = adamw_step(
            intake, intake_first, intake_second, intake_grad
        )
        outlet_next, outlet_momentum, outlet_variance = adamw_step(
            outlet, outlet_first, outlet_second, outlet_grad
        )
        expand_next, expand_momentum, expand_variance = adamw_step(
            expand, expand_first, expand_second, expand_grad
        )
        shrink_next, shrink_momentum, shrink_variance = adamw_step(
            shrink, shrink_first, shrink_second, shrink_grad
        )
        affine_next, affine_momentum, affine_variance = adamw_step(
            affine, affine_first, affine_second, affine_grad
        )
        offset_next, offset_momentum, offset_variance = adamw_step(
            offset, offset_first, offset_second, offset_grad
        )
        return (
            layer_out.reshape(tokens.shape),
            token_grad.reshape(cotangent.shape),
            intake_grad,
            outlet_grad,
            expand_grad,
            shrink_grad,
            affine_grad,
            offset_grad,
            intake_next,
            outlet_next,
            expand_next,
            shrink_next,
            affine_next,
            offset_next,
            intake_momentum,
            outlet_momentum,
            expand_momentum,
            shrink_momentum,
            affine_momentum,
            offset_momentum,
            intake_variance,
            outlet_variance,
            expand_variance,
            shrink_variance,
            affine_variance,
            offset_variance,
        )

    return body


def solution(mesh):
    rows = P("rep", "shard", None)
    params = (
        P(None, ("shard", "rep"), None),
        P(("shard", "rep"), None),
        P(("shard", "rep"), None),
        P(("shard", "rep"), None),
        P(None, ("shard", "rep")),
        P(("shard", "rep")),
    )
    return jax.shard_map(
        make_body(mesh.shape["shard"], mesh.shape["rep"]),
        mesh=mesh,
        in_specs=(rows, rows, P("rep", None)) + params * 3,
        out_specs=(rows, rows) + params * 4,
        check_vma=False,
    )
```

```python
import itertools
import math

import jax
import jax.numpy as jnp
from jax import lax
from jax.experimental import pallas as pl
from jax.experimental.pallas import tpu as pltpu
from jax.sharding import PartitionSpec as P

HEAD_DIM = 64


lr_rate = 0.03
beta_one = 0.9
beta_two = 0.95
adam_eps = 1e-08
weight_decay = 0.1
step_count = 3
norm_eps = 1e-05

f32 = jnp.float32
bf16 = jnp.bfloat16


def layer_norm(values_in):
    centred = values_in - jnp.mean(values_in, axis=-1, keepdims=True)
    inv_std = lax.rsqrt(jnp.mean(centred * centred, axis=-1, keepdims=True) + norm_eps)
    return (centred * inv_std, inv_std)


def norm_back(grad_normed, normed, inv_std):
    return inv_std * (
        grad_normed
        - jnp.mean(grad_normed, axis=-1, keepdims=True)
        - normed * jnp.mean(grad_normed * normed, axis=-1, keepdims=True)
    )


def gelu_value(hidden):
    return 0.5 * hidden * (1.0 + jax.scipy.special.erf(hidden / math.sqrt(2.0)))


def gelu_slope(hidden):
    return 0.5 * (1.0 + jax.scipy.special.erf(hidden / math.sqrt(2.0))) + hidden * jnp.exp(
        -0.5 * hidden * hidden
    ) / math.sqrt(2.0 * math.pi)


def adamw_step(weight, first_mom, second_mom, gradient):
    momentum = beta_one * first_mom + (1.0 - beta_one) * gradient
    variance = beta_two * second_mom + (1.0 - beta_two) * gradient * gradient
    fixed_mom = momentum / (1.0 - beta_one**step_count)
    fixed_var = variance / (1.0 - beta_two**step_count)
    return (
        weight - lr_rate * (fixed_mom / (jnp.sqrt(fixed_var) + adam_eps) + weight_decay * weight),
        momentum,
        variance,
    )


def dot_on(left_side, right_side, left_dim, right_dim):
    return lax.dot_general(
        left_side,
        right_side,
        (((left_dim,), (right_dim,)), ((), ())),
        preferred_element_type=f32,
    )


def dot_plain(left_side, right_side):
    return dot_on(left_side, right_side, 1, 0)


def dot_rows(left_side, right_side):
    return dot_on(left_side, right_side, 1, 1)


def dot_cols(left_side, right_side):
    return dot_on(left_side, right_side, 0, 0)


def masked_exp(query_head, key_head, same_doc):
    scores = dot_cols(key_head, query_head) * (1.0 / math.sqrt(HEAD_DIM))
    exp_scores = jnp.where(same_doc, jnp.exp(scores), 0.0)
    return exp_scores / jnp.sum(exp_scores, axis=0, keepdims=True)


def head_slices(head, heads, rows, stride, start):
    return [
        slice(base, base + rows)
        for base in range(head * stride + start, heads * stride * (HEAD_DIM // rows), heads * stride)
    ]


def read_head(ref, slices):
    return jnp.concatenate([ref[one, :] for one in slices], axis=0)


def write_head(ref, slices, value):
    rows = value.shape[0] // len(slices)
    for i, one in enumerate(slices):
        ref[one, :] = value[i * rows : (i + 1) * rows]


def attend_kernel(rows, inner_ref, seg_col_ref, seg_row_ref, out_ref):
    heads = out_ref.shape[0] // HEAD_DIM
    same_doc = seg_col_ref[...] == seg_row_ref[...]
    for head in range(heads):
        query, key, value = [
            read_head(inner_ref, head_slices(head, heads, rows, 3 * rows, i * rows))
            for i in range(3)
        ]
        probs = masked_exp(query, key, same_doc)
        attended = dot_plain(value, probs.astype(bf16)).astype(bf16)
        write_head(out_ref, head_slices(head, heads, rows, rows, 0), attended)


def attend_back_kernel(rows, inner_ref, grad_ref, seg_col_ref, seg_row_ref, out_ref, sum_ref):
    score_scale = 1.0 / math.sqrt(HEAD_DIM)
    heads = grad_ref.shape[0] // HEAD_DIM
    same_doc = seg_col_ref[...] == seg_row_ref[...]
    for head in range(heads):
        slots = [head_slices(head, heads, rows, 3 * rows, i * rows) for i in range(3)]
        query, key, value = [read_head(inner_ref, one) for one in slots]
        outer = head_slices(head, heads, rows, rows, 0)
        grad = read_head(grad_ref, outer)
        probs = masked_exp(query, key, same_doc)
        prob_grad = dot_cols(value, grad)
        row_dots = jnp.sum(probs * prob_grad, axis=0, keepdims=True)
        score_half = (probs * (prob_grad - row_dots)).astype(bf16)
        dq = dot_plain(key, score_half) * score_scale
        dk = dot_rows(query, score_half) * score_scale
        dv = dot_rows(grad, probs.astype(bf16))
        for one, value_out in zip(slots, (dq, dk, dv)):
            write_head(out_ref, one, value_out.astype(bf16))
        for column, value_out in enumerate((dq, dv)):
            sums = jnp.sum(value_out, axis=1, keepdims=True)
            for i, one in enumerate(outer):
                sum_ref[one, column : column + 1] = sums[i * rows : (i + 1) * rows]


def factor_rep(count, first):
    factors = [first]
    count //= first
    while count > 1:
        step = 4 if count % 4 == 0 else 2
        factors.append(step)
        count //= step
    return factors


def make_body(groups, replicas):
    shard_bits = [1 << i for i in range(groups.bit_length() - 1)]

    def swap(value, axis, count, bit):
        return lax.ppermute(value, axis, [(i, i ^ bit) for i in range(count)])

    slot_order = sorted(range(groups), key=lambda i: (i & 1, i))

    def gather_group(piece):
        pieces = {0: piece}
        for bit in reversed(shard_bits):
            for slot in list(pieces):
                pieces[slot ^ bit] = swap(pieces[slot], "shard", groups, bit)
        return [pieces[i] for i in slot_order]

    def scatter_group(near, far):
        total = near + swap(far.astype(bf16), "shard", groups, 1).astype(f32)
        for bit in reversed(shard_bits[1:]):
            half = total.shape[0] // 2
            came = swap(total[half:].astype(bf16), "shard", groups, bit)
            total = total[:half] + came.astype(f32)
        return total

    def body(
        tokens,
        cotangent,
        segment_ids,
        intake,
        outlet,
        expand,
        shrink,
        affine,
        offset,
        intake_first,
        outlet_first,
        expand_first,
        shrink_first,
        affine_first,
        offset_first,
        intake_second,
        outlet_second,
        expand_second,
        shrink_second,
        affine_second,
        offset_second,
    ):
        own_rows = tokens.shape[1]
        width = tokens.shape[2]
        seq_len = own_rows * groups
        head_cols = intake.shape[1] * replicas
        factors = factor_rep(replicas, head_cols // HEAD_DIM)
        strides = [math.prod(factors[i + 1 :]) for i in range(len(factors))]
        lead = factors[0]
        suffixes = list(itertools.product(*[range(f) for f in factors[1:]]))
        own_shard = lax.axis_index("shard")
        own_rep = lax.axis_index("rep")

        def shift(value, level, amount):
            pairs = []
            for r in range(replicas):
                coord = (r // strides[level]) % factors[level]
                moved = (coord + amount) % factors[level]
                pairs.append((r, r + (moved - coord) * strides[level]))
            return lax.ppermute(value, "rep", pairs)

        def gather_rep(piece):
            lead_parts = [piece] + [shift(piece, 0, k) for k in range(1, lead)]
            if len(factors) > 2:
                return gather_rest({(): jnp.concatenate(lead_parts, axis=0)})
            blocks = [lead_parts]
            for k in range(1, len(suffixes)):
                blocks.append([shift(v, 1, k) for v in lead_parts])
            return blocks

        def gather_rest(blocks):
            for level in range(1, len(factors)):
                joined = jnp.concatenate(list(blocks.values()), axis=0)
                grown = {s + (0,): v for s, v in blocks.items()}
                for k in range(1, factors[level]):
                    came = jnp.split(shift(joined, level, k), len(blocks))
                    grown.update({s + (k,): v for s, v in zip(blocks, came)})
                blocks = grown
            return [jnp.split(blocks[s], lead) for s in suffixes]

        def join(blocks, start, stop):
            return [jnp.concatenate([p[start:stop] for p in parts], axis=0) for parts in blocks]

        def add_up(blocks, start, stop):
            return sum(p[start:stop].astype(f32) for parts in blocks for p in parts)

        aligned = intake.shape[1] % 16 == 0
        head_rows = intake.shape[1] if aligned else HEAD_DIM

        def order_heads(blocks, kinds):
            joined = jnp.concatenate(blocks, axis=0)
            if not aligned:
                split = joined.reshape(len(suffixes), lead, kinds, -1, joined.shape[1])
                joined = split.transpose(1, 2, 0, 3, 4).reshape(joined.shape)
            return joined

        def by_suffix(left_side, right_side, kinds):
            if aligned:
                rows = left_side.shape[0] // len(suffixes)
                return [
                    dot_plain(left_side[i * rows : (i + 1) * rows], right_side)
                    for i in range(len(suffixes))
                ]
            product = dot_plain(left_side, right_side)
            split = product.reshape(lead, kinds, len(suffixes), -1, product.shape[1])
            split = split.transpose(2, 0, 1, 3, 4)
            return list(split.reshape(len(suffixes), -1, product.shape[1]))

        def scatter_rep(blocks, shared=None, units=None, parts=1):
            blocks = dict(zip(suffixes, blocks))
            if shared is not None:
                units = dict(zip(suffixes, units))

            def pack(pieces):
                if shared is None:
                    return pieces
                row = jnp.concatenate([units_now[s] for s in sorted(units_now)], axis=1)
                row = jnp.pad(row, ((0, 0), (0, width - row.shape[1])))
                tail = jnp.zeros((extra - shared.shape[0] - 1, width), f32)
                return pieces + [shared, row, tail]

            for level in reversed(range(1, len(factors))):
                merged = {s[:-1]: v for s, v in blocks.items() if s[-1] == 0}
                total_shared = shared
                if shared is not None:
                    total_units = {s[:-1]: v for s, v in units.items() if s[-1] == 0}
                for k in range(1, factors[level]):
                    units_now = {} if shared is None else {s: units[s + (k,)] for s in merged}
                    whole = pack([blocks[s + (k,)] for s in merged])
                    if shared is None and len(whole) == 1 and parts > 1:
                        cuts = jnp.split(whole[0], parts)
                        came = [shift(c.astype(bf16), level, -k) for c in cuts]
                        came = jnp.concatenate([c.astype(f32) for c in came], axis=0)
                    else:
                        whole = jnp.concatenate([w.astype(bf16) for w in whole], axis=0)
                        came = shift(whole, level, -k).astype(f32)
                    rows = next(iter(blocks.values())).shape[0]
                    for i, s in enumerate(list(merged)):
                        merged[s] = merged[s] + came[i * rows : (i + 1) * rows]
                    if shared is not None:
                        base = rows * len(merged)
                        total_shared = total_shared + came[base : base + shared.shape[0]]
                        row = came[base + shared.shape[0]][None]
                        size = next(iter(units.values())).shape[1]
                        for i, s in enumerate(sorted(merged)):
                            total_units[s] = total_units[s] + row[:, i * size : (i + 1) * size]
                blocks = merged
                if shared is not None:
                    shared, units = total_shared, total_units
            whole = blocks[()]
            rows = whole.shape[0] // lead
            total = whole[:rows]
            if shared is None:
                for k in range(1, lead):
                    came = shift(whole[k * rows : (k + 1) * rows].astype(bf16), 0, -k)
                    total = total + came.astype(f32)
                return total
            line = units[()]
            size = line.shape[1] // lead
            total_shared, total_units = shared, line[:, :size]
            for k in range(1, lead):
                units_now = {(): line[:, k * size : (k + 1) * size]}
                sent = pack([whole[k * rows : (k + 1) * rows]])
                sent = jnp.concatenate([w.astype(bf16) for w in sent], axis=0)
                came = shift(sent, 0, -k).astype(f32)
                total = total + came[:rows]
                total_shared = total_shared + came[rows : rows + shared.shape[0]]
                total_units = total_units + came[rows + shared.shape[0]][None, :size]
            return total, total_shared, total_units

        extra = 16
        own_cols = affine.shape[1]
        own_start = (own_shard * replicas + own_rep) * own_cols
        placed = lax.dynamic_update_slice(
            jnp.zeros((affine.shape[0], width), bf16), affine.astype(bf16), (0, own_start)
        )
        small_rows = affine.shape[0]
        unit_row = jnp.pad(
            offset.astype(bf16).reshape(1, -1),
            ((0, extra - small_rows - 1), (0, width - offset.shape[0])),
        )
        source = tokens.reshape(own_rows, width)
        intake_low = intake.astype(bf16).reshape(-1, width)
        intake_rows = intake_low.shape[0]
        blocks = gather_rep(jnp.concatenate([intake_low, placed, unit_row], axis=0))
        w_in = order_heads(join(blocks, 0, intake_rows), 3)
        own_coeffs = add_up(blocks, intake_rows, intake_rows + small_rows)
        unit_at = intake_rows + small_rows
        unit_bias = [
            jnp.concatenate([p[unit_at : unit_at + 1, : offset.shape[0]] for p in parts], axis=1)
            for parts in blocks
        ]
        unit_bias = [b.astype(f32) for b in unit_bias]

        token_parts = gather_group(
            jnp.concatenate([source, jnp.pad(placed, ((0, extra - small_rows), (0, 0)))], axis=0)
        )
        group_tokens = jnp.concatenate([p[:own_rows] for p in token_parts], axis=0)
        placed = sum(p[own_rows:].astype(f32) for p in token_parts).astype(bf16)

        out_rows = outlet.shape[0]
        wide_rows = expand.shape[0]
        blocks = gather_rep(
            jnp.concatenate([outlet.astype(bf16), placed, expand.astype(bf16)], axis=0)
        )
        w_out = order_heads(join(blocks, 0, out_rows), 1)
        coeffs = add_up(blocks, out_rows, out_rows + small_rows)
        w_expand = join(blocks, out_rows + extra, out_rows + extra + wide_rows)
        w_shrink = join(gather_rep(shrink.astype(bf16)), 0, wide_rows)

        index = lax.broadcasted_iota(jnp.int32, (head_cols, 1), 0)
        part_rows = intake.shape[1]
        if aligned:
            suffix_index = index // (lead * part_rows)
            lead_index = index // part_rows % lead
        else:
            lead_index = index // HEAD_DIM
            suffix_index = index // part_rows % len(suffixes)
        slot_index = lead_index * len(suffixes) + suffix_index
        feature_rep = jnp.zeros_like(index)
        for stride, factor in zip(strides, factors):
            slot = (slot_index // stride) % factor
            coord = (own_rep // stride) % factor
            feature_rep = feature_rep + ((coord - slot + factor) % factor) * stride
        feature = (own_shard * replicas + feature_rep) * own_cols + index % own_cols
        picks = feature == lax.broadcasted_iota(jnp.int32, (head_cols, width), 1)
        head_bias = dot_rows(picks.astype(bf16), own_coeffs[0:2].astype(bf16))
        head_bias = head_bias.reshape(-1, head_rows, 2)
        no_bias = jnp.zeros((head_bias.shape[0], head_rows, 1), f32)
        inner_bias = jnp.concatenate([head_bias[:, :, 0:1], no_bias, head_bias[:, :, 1:2]], axis=1)

        every_seg = segment_ids.reshape(seq_len)
        seg_slots = jnp.concatenate(
            [
                lax.dynamic_slice_in_dim(every_seg, (own_shard ^ k) * own_rows, own_rows)
                for k in slot_order
            ]
        )
        seg_col = seg_slots.reshape(seq_len, 1)
        seg_row = seg_slots.reshape(1, seq_len)

        inner = (dot_rows(w_in, group_tokens) + inner_bias.reshape(-1, 1)).astype(bf16)
        attended = pl.pallas_call(
            lambda *refs: attend_kernel(head_rows, *refs),
            out_shape=jax.ShapeDtypeStruct((head_cols, seq_len), bf16),
            name="attend",
        )(inner, seg_col, seg_row)

        half = seq_len // 2
        far_out = dot_cols(attended[:, half:], w_out)
        near_out = dot_cols(attended[:, :half], w_out)
        attn_out = scatter_group(near_out, far_out)
        resid_one = source.astype(f32) + attn_out + coeffs[2]
        normed_one, inv_one = layer_norm(resid_one)
        mixed_one = normed_one * (1.0 + coeffs[3]) + coeffs[4]
        inner_in = mixed_one.astype(bf16)
        group_in = jnp.concatenate(gather_group(inner_in), axis=0)
        hidden = [dot_rows(group_in, w) + b for w, b in zip(w_expand, unit_bias)]
        act_half = [gelu_value(h).astype(bf16) for h in hidden]
        far_out = sum(dot_plain(a[half:], w) for a, w in zip(act_half, w_shrink))
        near_out = sum(dot_plain(a[:half], w) for a, w in zip(act_half, w_shrink))
        ffn_out = scatter_group(near_out, far_out)
        resid_two = mixed_one + ffn_out + coeffs[5]
        normed_two, inv_two = layer_norm(resid_two)
        layer_out = (normed_two * (1.0 + coeffs[6]) + coeffs[7]).astype(bf16)

        out_grad = cotangent.reshape(own_rows, width).astype(f32)
        grad_two = norm_back(out_grad * (1.0 + coeffs[6]), normed_two, inv_two)
        group_grad = jnp.concatenate(gather_group(grad_two.astype(bf16)), axis=0)
        gain_two = jnp.sum(out_grad * normed_two, axis=0)
        shift_two = jnp.sum(out_grad, axis=0)
        grad_hidden = [
            dot_rows(group_grad, w) * gelu_slope(h) for w, h in zip(w_shrink, hidden)
        ]
        hidden_half = [g.astype(bf16) for g in grad_hidden]
        far_out = sum(dot_plain(g[half:], w) for g, w in zip(hidden_half, w_expand))
        near_out = sum(dot_plain(g[:half], w) for g, w in zip(hidden_half, w_expand))
        grad_inner = scatter_group(near_out, far_out)
        shrink_grad = scatter_rep([dot_cols(a, group_grad) for a in act_half], parts=2)
        expand_grad = scatter_rep([dot_cols(g, group_in) for g in hidden_half])
        unit_sums = [jnp.sum(g, axis=0, keepdims=True) for g in grad_hidden]
        bias_two = jnp.sum(group_grad.astype(f32), axis=0)
        grad_mixed = grad_two + grad_inner
        grad_one = norm_back(grad_mixed * (1.0 + coeffs[3]), normed_one, inv_one)
        gain_one = jnp.sum(grad_mixed * normed_one, axis=0)
        shift_one = jnp.sum(grad_mixed, axis=0)
        sums = jnp.stack([gain_one, shift_one, gain_two, shift_two])
        sums = jnp.pad(sums, ((0, extra - sums.shape[0]), (0, 0)))
        one_parts = gather_group(
            jnp.concatenate([grad_one.astype(bf16), sums.astype(bf16)], axis=0)
        )
        group_one = jnp.concatenate([p[:own_rows] for p in one_parts], axis=0)
        attend_grad = dot_rows(w_out, group_one).astype(bf16)
        sums = sum(p[own_rows:].astype(f32) for p in one_parts)
        bias_out = jnp.sum(group_one.astype(f32), axis=0)
        outlet_grad = scatter_rep(by_suffix(attended, group_one, 1))
        inner_grad, head_sums = pl.pallas_call(
            lambda *refs: attend_back_kernel(head_rows, *refs),
            out_shape=(
                jax.ShapeDtypeStruct(inner.shape, bf16),
                jax.ShapeDtypeStruct((head_cols, 2), f32),
            ),
            name="attend_back",
        )(inner, attend_grad, seg_col, seg_row)
        far_out = dot_cols(inner_grad[:, half:], w_in)
        near_out = dot_cols(inner_grad[:, :half], w_in)
        token_grad = (grad_one + scatter_group(near_out, far_out)).astype(bf16)
        bias_rows = lax.dot_general(
            head_sums,
            picks.astype(f32),
            (((0,), (0,)), ((), ())),
            precision=lax.Precision.HIGHEST,
            preferred_element_type=f32,
        )
        shared = jnp.concatenate(
            [bias_rows, jnp.stack([bias_out, sums[0], sums[1], bias_two, sums[2], sums[3]])], axis=0
        )
        intake_grad, affine_full, offset_grad = scatter_rep(
            by_suffix(inner_grad, group_tokens, 3), shared, unit_sums
        )
        intake_grad = intake_grad.reshape(intake.shape)
        offset_grad = offset_grad.reshape(offset.shape)
        affine_grad = lax.dynamic_slice(affine_full, (0, own_start), affine.shape)

        intake_next, intake_momentum, intake_variance = adamw_step(
            intake, intake_first, intake_second, intake_grad
        )
        outlet_next, outlet_momentum, outlet_variance = adamw_step(
            outlet, outlet_first, outlet_second, outlet_grad
        )
        expand_next, expand_momentum, expand_variance = adamw_step(
            expand, expand_first, expand_second, expand_grad
        )
        shrink_next, shrink_momentum, shrink_variance = adamw_step(
            shrink, shrink_first, shrink_second, shrink_grad
        )
        affine_next, affine_momentum, affine_variance = adamw_step(
            affine, affine_first, affine_second, affine_grad
        )
        offset_next, offset_momentum, offset_variance = adamw_step(
            offset, offset_first, offset_second, offset_grad
        )
        return (
            layer_out.reshape(tokens.shape),
            token_grad.reshape(cotangent.shape),
            intake_grad,
            outlet_grad,
            expand_grad,
            shrink_grad,
            affine_grad,
            offset_grad,
            intake_next,
            outlet_next,
            expand_next,
            shrink_next,
            affine_next,
            offset_next,
            intake_momentum,
            outlet_momentum,
            expand_momentum,
            shrink_momentum,
            affine_momentum,
            offset_momentum,
            intake_variance,
            outlet_variance,
            expand_variance,
            shrink_variance,
            affine_variance,
            offset_variance,
        )

    return body


def solution(mesh):
    rows = P("rep", "shard", None)
    params = (
        P(None, ("shard", "rep"), None),
        P(("shard", "rep"), None),
        P(("shard", "rep"), None),
        P(("shard", "rep"), None),
        P(None, ("shard", "rep")),
        P(("shard", "rep")),
    )
    return jax.shard_map(
        make_body(mesh.shape["shard"], mesh.shape["rep"]),
        mesh=mesh,
        in_specs=(rows, rows, P("rep", None)) + params * 3,
        out_specs=(rows, rows) + params * 4,
        check_vma=False,
    )
```

```python
import itertools
import math

import jax
import jax.numpy as jnp
from jax import lax
from jax.experimental import pallas as pl
from jax.experimental.pallas import tpu as pltpu
from jax.sharding import PartitionSpec as P


HEAD_DIM = 64


lr_rate = 0.03
beta_one = 0.9
beta_two = 0.95
adam_eps = 1e-08
weight_decay = 0.1
step_count = 3
norm_eps = 1e-05

f32 = jnp.float32
bf16 = jnp.bfloat16


def layer_norm(values_in):
    centred = values_in - jnp.mean(values_in, axis=-1, keepdims=True)
    inv_std = lax.rsqrt(jnp.mean(centred * centred, axis=-1, keepdims=True) + norm_eps)
    return (centred * inv_std, inv_std)


def norm_back(grad_normed, normed, inv_std):
    return inv_std * (
        grad_normed
        - jnp.mean(grad_normed, axis=-1, keepdims=True)
        - normed * jnp.mean(grad_normed * normed, axis=-1, keepdims=True)
    )


def adamw_step(weight, first_mom, second_mom, gradient):
    momentum = beta_one * first_mom + (1.0 - beta_one) * gradient
    variance = beta_two * second_mom + (1.0 - beta_two) * gradient * gradient
    fixed_mom = momentum / (1.0 - beta_one**step_count)
    fixed_var = variance / (1.0 - beta_two**step_count)
    return (
        weight - lr_rate * (fixed_mom / (jnp.sqrt(fixed_var) + adam_eps) + weight_decay * weight),
        momentum,
        variance,
    )


def dot_on(left_side, right_side, left_dim, right_dim):
    return lax.dot_general(
        left_side,
        right_side,
        (((left_dim,), (right_dim,)), ((), ())),
        preferred_element_type=f32,
    )


def dot_plain(left_side, right_side):
    return dot_on(left_side, right_side, 1, 0)


def dot_rows(left_side, right_side):
    return dot_on(left_side, right_side, 1, 1)


def dot_cols(left_side, right_side):
    return dot_on(left_side, right_side, 0, 0)


def masked_exp(query_head, key_head, same_doc):
    scores = dot_cols(key_head, query_head) * (1.0 / math.sqrt(HEAD_DIM))
    exp_scores = jnp.where(same_doc, jnp.exp(scores), 0.0)
    return exp_scores / jnp.sum(exp_scores, axis=0, keepdims=True)


def head_slices(head, heads, rows, stride, start):
    return [
        slice(base, base + rows)
        for base in range(head * stride + start, heads * stride * (HEAD_DIM // rows), heads * stride)
    ]


def read_head(ref, slices):
    return jnp.concatenate([ref[one, :] for one in slices], axis=0)


def write_head(ref, slices, value):
    rows = value.shape[0] // len(slices)
    for i, one in enumerate(slices):
        ref[one, :] = value[i * rows : (i + 1) * rows]


def fill(ref, pieces, start, stop):
    rows = stop - start
    for i, piece in enumerate(pieces):
        ref[i * rows : (i + 1) * rows, :] = piece[start:stop, :]


def split_out(far_ref, near_ref, make):
    half = near_ref.shape[0]
    far_ref[...] = make(slice(half, 2 * half)).astype(bf16)
    near_ref[...] = make(slice(0, half))


def attend_kernel(rows, in_rows, out_rows, unit_cols, count, *refs):
    pieces, refs = refs[:count], refs[count:]
    tokens, refs = refs[:-12], refs[-12:]
    picks_ref, seg_col_ref, seg_row_ref, *refs = refs
    w_in_ref, w_out_ref, group_ref, inner_ref, out_ref, coeff_ref, unit_ref, far_ref, near_ref = refs
    fill(w_in_ref, pieces, 0, in_rows)
    fill(w_out_ref, pieces, in_rows, in_rows + out_rows)
    fill(group_ref, tokens, 0, group_ref.shape[0] // len(tokens))
    small = [p[in_rows + out_rows :, :].astype(f32) for p in pieces]
    total = sum(small).astype(bf16)
    coeff_ref[...] = total
    unit_at = total.shape[0] // 2
    for i, one in enumerate(small):
        unit_ref[:, i * unit_cols : (i + 1) * unit_cols] = one[unit_at : unit_at + 1, :unit_cols]
    bias = dot_rows(picks_ref[...], total)
    product = dot_rows(w_in_ref[...], group_ref[...])
    heads = out_ref.shape[0] // HEAD_DIM
    blocks = HEAD_DIM // rows
    for slot in range(heads * blocks):
        base = slot * 3 * rows
        own = slice(slot * rows, (slot + 1) * rows)
        for i, add in enumerate((bias[own, 0:1], 0.0, bias[own, 1:2])):
            part = slice(base + i * rows, base + (i + 1) * rows)
            inner_ref[part, :] = (product[part] + add).astype(bf16)
    same_doc = seg_col_ref[...] == seg_row_ref[...]
    for head in range(heads):
        query, key, value = [
            read_head(inner_ref, head_slices(head, heads, rows, 3 * rows, i * rows))
            for i in range(3)
        ]
        probs = masked_exp(query, key, same_doc)
        attended = dot_plain(value, probs.astype(bf16)).astype(bf16)
        write_head(out_ref, head_slices(head, heads, rows, rows, 0), attended)
    split_out(far_ref, near_ref, lambda cols: dot_cols(out_ref[:, cols], w_out_ref[...]))


def units_kernel(start, stop, count, parts, *refs):
    pieces, refs = refs[:count], refs[count:]
    group, refs = refs[: -(parts + 4)], refs[-(parts + 4) :]
    unit_ref, w_ref, group_ref, slope_ref, *act_refs = refs
    fill(w_ref, pieces, start, stop)
    fill(group_ref, group, 0, group_ref.shape[0] // len(group))
    cols = act_refs[0].shape[1]
    for i, act_ref in enumerate(act_refs):
        own = slice(i * cols, (i + 1) * cols)
        hidden = dot_rows(group_ref[...], w_ref[own, :]) + unit_ref[:, own]
        bell = 0.5 * (1.0 + lax.erf(hidden * (1.0 / math.sqrt(2.0))))
        act_ref[...] = (hidden * bell).astype(bf16)
        slope = bell + hidden * jnp.exp(-0.5 * hidden * hidden) * (1.0 / math.sqrt(2.0 * math.pi))
        slope_ref[:, own] = slope


def shrink_kernel(count, *refs):
    pieces, refs = refs[:count], refs[count:]
    acts, (w_ref, far_ref, near_ref) = refs[:-3], refs[-3:]
    fill(w_ref, pieces, 0, pieces[0].shape[0])
    cols = acts[0].shape[1]

    def make(rows):
        terms = [
            dot_plain(act[rows, :], w_ref[i * cols : (i + 1) * cols, :])
            for i, act in enumerate(acts)
        ]
        return sum(terms[1:], terms[0])

    split_out(far_ref, near_ref, make)


def units_back_kernel(count, *refs):
    grads, refs = refs[:count], refs[count:]
    w_shrink_ref, w_expand_ref, slope_ref, group_ref, bias_ref, sum_ref, far_ref, near_ref = refs[:8]
    back_refs = refs[8:]
    fill(group_ref, grads, 0, grads[0].shape[0])
    cols = back_refs[0].shape[1]
    for i, back_ref in enumerate(back_refs):
        own = slice(i * cols, (i + 1) * cols)
        back = dot_rows(group_ref[...], w_shrink_ref[own, :]) * slope_ref[:, own]
        back_ref[...] = back.astype(bf16)
        sum_ref[:, own] = jnp.sum(back, axis=0, keepdims=True)

    def make(rows):
        terms = [
            dot_plain(back[rows, :], w_expand_ref[i * cols : (i + 1) * cols, :])
            for i, back in enumerate(back_refs)
        ]
        return sum(terms[1:], terms[0])

    split_out(far_ref, near_ref, make)
    bias_ref[...] = jnp.sum(group_ref[...].astype(f32), axis=0, keepdims=True)


def attend_back_kernel(rows, count, *refs):
    grads, refs = refs[:count], refs[count:]
    inner_ref, w_in_ref, w_out_ref, seg_col_ref, seg_row_ref = refs[:5]
    group_ref, shared_ref, out_ref, sum_ref, far_ref, near_ref, grad_ref = refs[5:]
    score_scale = 1.0 / math.sqrt(HEAD_DIM)
    own_rows = group_ref.shape[0] // count
    fill(group_ref, grads, 0, own_rows)
    grad_ref[...] = dot_rows(w_out_ref[...], group_ref[...]).astype(bf16)
    heads = grad_ref.shape[0] // HEAD_DIM
    same_doc = seg_col_ref[...] == seg_row_ref[...]
    for head in range(heads):
        slots = [head_slices(head, heads, rows, 3 * rows, i * rows) for i in range(3)]
        query, key, value = [read_head(inner_ref, one) for one in slots]
        outer = head_slices(head, heads, rows, rows, 0)
        grad = read_head(grad_ref, outer)
        probs = masked_exp(query, key, same_doc)
        prob_grad = dot_cols(value, grad)
        row_dots = jnp.sum(probs * prob_grad, axis=0, keepdims=True)
        score_half = (probs * (prob_grad - row_dots)).astype(bf16)
        dq = dot_plain(key, score_half) * score_scale
        dk = dot_rows(query, score_half) * score_scale
        dv = dot_rows(grad, probs.astype(bf16))
        for one, value_out in zip(slots, (dq, dk, dv)):
            write_head(out_ref, one, value_out.astype(bf16))
        for column, value_out in enumerate((dq, dv)):
            sums = jnp.sum(value_out, axis=1, keepdims=True)
            for i, one in enumerate(outer):
                sum_ref[one, column : column + 1] = sums[i * rows : (i + 1) * rows]
    split_out(far_ref, near_ref, lambda cols: dot_cols(out_ref[:, cols], w_in_ref[...]))
    bias = jnp.sum(group_ref[...].astype(f32), axis=0, keepdims=True)
    shared_ref[...] = sum(g[own_rows:, :].astype(f32) for g in grads)
    shared_ref[shared_ref.shape[0] - 1 :, :] = bias


def factor_rep(count, first):
    factors = [first]
    count //= first
    while count > 1:
        step = 4 if count % 4 == 0 else 2
        factors.append(step)
        count //= step
    return factors


def make_body(groups, replicas):
    shard_bits = [1 << i for i in range(groups.bit_length() - 1)]

    def swap(value, bit):
        return lax.ppermute(value, "shard", [(i, i ^ bit) for i in range(groups)])

    slot_order = sorted(range(groups), key=lambda i: (i & 1, i))

    def gather_group(piece):
        pieces = {0: piece}
        for bit in reversed(shard_bits):
            for slot in list(pieces):
                pieces[slot ^ bit] = swap(pieces[slot], bit)
        return [pieces[i] for i in slot_order]

    def scatter_group(near, far):
        total = near + swap(far, 1).astype(f32)
        for bit in reversed(shard_bits[1:]):
            half = total.shape[0] // 2
            came = swap(total[half:].astype(bf16), bit)
            total = total[:half] + came.astype(f32)
        return total

    def body(
        tokens,
        cotangent,
        segment_ids,
        intake,
        outlet,
        expand,
        shrink,
        affine,
        offset,
        intake_first,
        outlet_first,
        expand_first,
        shrink_first,
        affine_first,
        offset_first,
        intake_second,
        outlet_second,
        expand_second,
        shrink_second,
        affine_second,
        offset_second,
    ):
        own_rows = tokens.shape[1]
        width = tokens.shape[2]
        seq_len = own_rows * groups
        head_cols = intake.shape[1] * replicas
        factors = factor_rep(replicas, head_cols // HEAD_DIM)
        strides = [math.prod(factors[i + 1 :]) for i in range(len(factors))]
        lead = factors[0]
        suffixes = list(itertools.product(*[range(f) for f in factors[1:]]))
        own_shard = lax.axis_index("shard")
        own_rep = lax.axis_index("rep")

        bulk = len(factors) > 2
        aligned = intake.shape[1] % 16 == 0
        head_rows = intake.shape[1] if aligned else HEAD_DIM

        def shift(value, level, amount):
            pairs = []
            for r in range(replicas):
                coord = (r // strides[level]) % factors[level]
                moved = (coord + amount) % factors[level]
                pairs.append((r, r + (moved - coord) * strides[level]))
            return lax.ppermute(value, "rep", pairs)

        def gather_rep(piece):
            parts = [piece] + [shift(piece, 0, k) for k in range(1, lead)]
            if bulk:
                return gather_rest({(): jnp.concatenate(parts, axis=0)})
            blocks = list(parts)
            for k in range(1, len(suffixes)):
                blocks += [shift(v, 1, k) for v in parts]
            return blocks

        def gather_rest(blocks):
            for level in range(1, len(factors)):
                joined = jnp.concatenate(list(blocks.values()), axis=0)
                grown = {s + (0,): v for s, v in blocks.items()}
                for k in range(1, factors[level]):
                    came = jnp.split(shift(joined, level, k), len(blocks))
                    grown.update({s + (k,): v for s, v in zip(blocks, came)})
                blocks = grown
            return [p for s in suffixes for p in jnp.split(blocks[s], lead)]

        def join(pieces, start, stop):
            return jnp.concatenate([p[start:stop] for p in pieces], axis=0)

        def order_heads(joined, kinds):
            split = joined.reshape(len(suffixes), lead, kinds, -1, joined.shape[1])
            return split.transpose(1, 2, 0, 3, 4).reshape(joined.shape)

        def by_suffix(left_side, right_side, kinds, parts):
            if aligned:
                count = len(suffixes) * parts
                rows = left_side.shape[0] // count
                products = [
                    dot_plain(left_side[i * rows : (i + 1) * rows], right_side)
                    for i in range(count)
                ]
                return [products[i * parts : (i + 1) * parts] for i in range(len(suffixes))]
            product = dot_plain(left_side, right_side)
            split = product.reshape(lead, kinds, len(suffixes), -1, product.shape[1])
            split = split.transpose(2, 0, 1, 3, 4)
            return [[p] for p in split.reshape(len(suffixes), -1, product.shape[1])]

        def scatter_rep(blocks, shared=None, units=None):
            if bulk:
                blocks = [[jnp.concatenate(parts, axis=0)] for parts in blocks]
            blocks = dict(zip(suffixes, blocks))
            units = {} if shared is None else dict(zip(suffixes, units))

            def pack(pieces, line):
                if line is None:
                    return jnp.concatenate([p.astype(bf16) for p in pieces], axis=0)
                line = jnp.pad(line, ((0, extra - small_rows - 1), (0, width - line.shape[1])))
                joined = [p.astype(bf16) for p in [*pieces, shared, line]]
                return jnp.concatenate(joined, axis=0)

            for level in reversed(range(1, len(factors))):
                merged = {s[:-1]: list(v) for s, v in blocks.items() if s[-1] == 0}
                lines = {s[:-1]: v for s, v in units.items() if s[-1] == 0}
                total = shared
                for k in range(1, factors[level]):
                    for part in reversed(range(len(next(iter(merged.values()))))):
                        line = None
                        if shared is not None and part == 0:
                            line = jnp.concatenate([units[s + (k,)] for s in merged], axis=1)
                        sent = pack([blocks[s + (k,)][part] for s in merged], line)
                        came = shift(sent, level, -k).astype(f32)
                        rows = blocks[next(iter(blocks))][part].shape[0]
                        for i, s in enumerate(merged):
                            merged[s][part] = merged[s][part] + came[i * rows : (i + 1) * rows]
                        if line is not None:
                            at = came.shape[0] - extra
                            total = total + came[at : at + small_rows]
                            size = line.shape[1] // len(merged)
                            row = came[at + small_rows][None]
                            for i, s in enumerate(merged):
                                lines[s] = lines[s] + row[:, i * size : (i + 1) * size]
                blocks, shared, units = merged, total, lines
            parts = blocks[()]
            per_part = lead // len(parts)
            rows = parts[0].shape[0] // per_part

            def slot(k):
                at = k % per_part * rows
                return parts[k // per_part][at : at + rows]

            result, total = slot(0), shared
            if shared is not None:
                size = units[()].shape[1] // lead
                line_total = units[()][:, :size]
            for k in range(1, lead):
                line = None if shared is None else units[()][:, k * size : (k + 1) * size]
                came = shift(pack([slot(k)], line), 0, -k).astype(f32)
                result = result + came[:rows]
                if shared is not None:
                    total = total + came[rows : rows + small_rows]
                    line_total = line_total + came[rows + small_rows][None, :size]
            return result if shared is None else (result, total, line_total)

        extra = 16
        own_cols = affine.shape[1]
        own_start = (own_shard * replicas + own_rep) * own_cols
        small_rows = affine.shape[0]
        placed = lax.dynamic_update_slice(
            jnp.zeros((small_rows, width), bf16), affine.astype(bf16), (0, own_start)
        )
        unit_row = jnp.pad(
            offset.astype(bf16).reshape(1, -1),
            ((0, extra - small_rows - 1), (0, width - offset.shape[0])),
        )
        source = tokens.reshape(own_rows, width)
        own_small = jnp.pad(placed, ((0, extra - small_rows), (0, 0)))
        token_parts = gather_group(jnp.concatenate([source, own_small], axis=0))

        intake_low = intake.astype(bf16).reshape(-1, width)
        in_rows = intake_low.shape[0]
        out_rows = outlet.shape[0]
        wide_rows = expand.shape[0]
        pieces = gather_rep(
            jnp.concatenate([intake_low, outlet.astype(bf16), placed, unit_row], axis=0)
        )
        placed_group = sum(p[own_rows:].astype(f32) for p in token_parts).astype(bf16)
        wide_pieces = gather_rep(jnp.concatenate([expand.astype(bf16), placed_group], axis=0))
        shrink_pieces = gather_rep(shrink.astype(bf16))
        unit_cols = offset.shape[0]
        if not aligned:
            at = in_rows + out_rows
            line = jnp.concatenate([p[at + small_rows :][:1, :unit_cols] for p in pieces], axis=1)
            line = jnp.pad(line, ((0, extra - small_rows - 1), (0, width - line.shape[1])))
            placed_all = sum(p[at : at + small_rows].astype(f32) for p in pieces).astype(bf16)
            w_in = order_heads(join(pieces, 0, in_rows), 3)
            w_out = order_heads(join(pieces, in_rows, at), 1)
            pieces = [jnp.concatenate([w_in, w_out, placed_all, line], axis=0)]
            wide_joined = join(wide_pieces, 0, wide_rows)
            placed_all = sum(p[wide_rows:].astype(f32) for p in wide_pieces).astype(bf16)
            wide_pieces = [jnp.concatenate([wide_joined, placed_all], axis=0)]
            shrink_pieces = [join(shrink_pieces, 0, wide_rows)]
            in_rows, out_rows = in_rows * replicas, out_rows * replicas
            wide_rows, unit_cols = wide_rows * replicas, unit_cols * replicas
        coeffs = sum(p[wide_rows : wide_rows + small_rows].astype(f32) for p in wide_pieces)
        units = wide_rows * len(wide_pieces)

        index = lax.broadcasted_iota(jnp.int32, (head_cols, 1), 0)
        part_rows = intake.shape[1]
        if aligned:
            suffix_index = index // (lead * part_rows)
            lead_index = index // part_rows % lead
        else:
            lead_index = index // HEAD_DIM
            suffix_index = index // part_rows % len(suffixes)
        slot_index = lead_index * len(suffixes) + suffix_index
        feature_rep = jnp.zeros_like(index)
        for stride, factor in zip(strides, factors):
            slot_at = (slot_index // stride) % factor
            coord = (own_rep // stride) % factor
            feature_rep = feature_rep + ((coord - slot_at + factor) % factor) * stride
        feature = (own_shard * replicas + feature_rep) * own_cols + index % own_cols
        picks = feature == lax.broadcasted_iota(jnp.int32, (head_cols, width), 1)

        every_seg = segment_ids.reshape(seq_len)
        seg_slots = jnp.concatenate(
            [
                lax.dynamic_slice_in_dim(every_seg, (own_shard ^ k) * own_rows, own_rows)
                for k in slot_order
            ]
        )
        seg_col = seg_slots.reshape(seq_len, 1)
        seg_row = seg_slots.reshape(1, seq_len)

        def call(kernel, outs, *operands, scratch=()):
            return pl.pallas_call(
                kernel,
                out_shape=[jax.ShapeDtypeStruct(shape, dtype) for shape, dtype in outs],
                scratch_shapes=[pltpu.VMEM(shape, dtype) for shape, dtype in scratch],
            )(*operands)

        half = seq_len // 2
        full = (seq_len, width)
        two_halves = [((half, width), bf16), ((half, width), f32)]
        w_in, w_out, group_tokens, inner, attended, _, unit_bias, far, near = call(
            lambda *refs: attend_kernel(head_rows, in_rows, out_rows, unit_cols, len(pieces), *refs),
            [
                ((3 * head_cols, width), bf16),
                ((head_cols, width), bf16),
                (full, bf16),
                ((3 * head_cols, seq_len), bf16),
                ((head_cols, seq_len), bf16),
                ((extra, width), bf16),
                ((1, units), f32),
                *two_halves,
            ],
            *pieces,
            *token_parts,
            picks.astype(bf16),
            seg_col,
            seg_row,
        )
        attn_out = scatter_group(near, far)
        resid_one = source.astype(f32) + attn_out + coeffs[2]
        normed_one, inv_one = layer_norm(resid_one)
        mixed_one = normed_one * (1.0 + coeffs[3]) + coeffs[4]
        inner_parts = gather_group(mixed_one.astype(bf16))
        parts = 2
        count = parts * (1 if bulk else len(suffixes))
        thin = [((seq_len, units // count), bf16)] * count
        w_expand, group_in, slope, *acts = call(
            lambda *refs: units_kernel(0, wide_rows, len(wide_pieces), count, *refs),
            [((units, width), bf16), (full, bf16), ((seq_len, units), f32), *thin],
            *wide_pieces,
            *inner_parts,
            unit_bias,
        )
        w_shrink, far, near = call(
            lambda *refs: shrink_kernel(len(shrink_pieces), *refs),
            [((units, width), bf16), *two_halves],
            *shrink_pieces,
            *acts,
        )
        ffn_out = scatter_group(near, far)
        resid_two = mixed_one + ffn_out + coeffs[5]
        normed_two, inv_two = layer_norm(resid_two)
        layer_out = (normed_two * (1.0 + coeffs[6]) + coeffs[7]).astype(bf16)

        out_grad = cotangent.reshape(own_rows, width).astype(f32)
        grad_two = norm_back(out_grad * (1.0 + coeffs[6]), normed_two, inv_two)
        grad_parts = gather_group(grad_two.astype(bf16))
        gain_two = jnp.sum(out_grad * normed_two, axis=0)
        shift_two = jnp.sum(out_grad, axis=0)
        group_grad, bias_two, unit_sums, far, near, *backs = call(
            lambda *refs: units_back_kernel(groups, *refs),
            [(full, bf16), ((1, width), f32), ((1, units), f32), *two_halves, *thin],
            *grad_parts,
            w_shrink,
            w_expand,
            slope,
        )

        def unit_blocks(lefts, right_side):
            if bulk:
                product = dot_cols(jnp.concatenate(lefts, axis=1), right_side)
                return [[p] for p in jnp.split(product, len(suffixes))]
            products = [dot_cols(left, right_side) for left in lefts]
            return [products[i * parts : (i + 1) * parts] for i in range(len(suffixes))]

        shrink_grad = scatter_rep(unit_blocks(acts, group_grad))
        grad_inner = scatter_group(near, far)
        expand_grad = scatter_rep(unit_blocks(backs, group_in))
        grad_mixed = grad_two + grad_inner
        grad_one = norm_back(grad_mixed * (1.0 + coeffs[3]), normed_one, inv_one)
        gain_one = jnp.sum(grad_mixed * normed_one, axis=0)
        shift_one = jnp.sum(grad_mixed, axis=0)
        sums = jnp.stack([gain_one, shift_one, gain_two, shift_two])
        sums = jnp.pad(sums, ((0, extra - sums.shape[0]), (0, 0)))
        one_parts = gather_group(
            jnp.concatenate([grad_one.astype(bf16), sums.astype(bf16)], axis=0)
        )
        group_one, sums, inner_grad, head_sums, far, near = call(
            lambda *refs: attend_back_kernel(head_rows, groups, *refs),
            [
                (full, bf16),
                ((extra, width), f32),
                (inner.shape, bf16),
                ((head_cols, 2), f32),
                *two_halves,
            ],
            *one_parts,
            inner,
            w_in,
            w_out,
            seg_col,
            seg_row,
            scratch=[((head_cols, seq_len), bf16)],
        )
        token_grad = (grad_one + scatter_group(near, far)).astype(bf16)
        outlet_grad = scatter_rep(by_suffix(attended, group_one, 1, 1))
        bias_rows = lax.dot_general(
            head_sums,
            picks.astype(f32),
            (((0,), (0,)), ((), ())),
            precision=lax.Precision.HIGHEST,
            preferred_element_type=f32,
        )
        shared = jnp.concatenate(
            [bias_rows, sums[extra - 1 :], sums[0:2], bias_two, sums[2:4]], axis=0
        )
        intake_grad, affine_full, offset_grad = scatter_rep(
            by_suffix(inner_grad, group_tokens, 3, parts),
            shared,
            jnp.split(unit_sums, len(suffixes), axis=1),
        )
        intake_grad = intake_grad.reshape(intake.shape)
        offset_grad = offset_grad.reshape(offset.shape)
        affine_grad = lax.dynamic_slice(affine_full, (0, own_start), affine.shape)

        intake_next, intake_momentum, intake_variance = adamw_step(
            intake, intake_first, intake_second, intake_grad
        )
        outlet_next, outlet_momentum, outlet_variance = adamw_step(
            outlet, outlet_first, outlet_second, outlet_grad
        )
        expand_next, expand_momentum, expand_variance = adamw_step(
            expand, expand_first, expand_second, expand_grad
        )
        shrink_next, shrink_momentum, shrink_variance = adamw_step(
            shrink, shrink_first, shrink_second, shrink_grad
        )
        affine_next, affine_momentum, affine_variance = adamw_step(
            affine, affine_first, affine_second, affine_grad
        )
        offset_next, offset_momentum, offset_variance = adamw_step(
            offset, offset_first, offset_second, offset_grad
        )
        return (
            layer_out.reshape(tokens.shape),
            token_grad.reshape(cotangent.shape),
            intake_grad,
            outlet_grad,
            expand_grad,
            shrink_grad,
            affine_grad,
            offset_grad,
            intake_next,
            outlet_next,
            expand_next,
            shrink_next,
            affine_next,
            offset_next,
            intake_momentum,
            outlet_momentum,
            expand_momentum,
            shrink_momentum,
            affine_momentum,
            offset_momentum,
            intake_variance,
            outlet_variance,
            expand_variance,
            shrink_variance,
            affine_variance,
            offset_variance,
        )

    return body


def solution(mesh):
    rows = P("rep", "shard", None)
    params = (
        P(None, ("shard", "rep"), None),
        P(("shard", "rep"), None),
        P(("shard", "rep"), None),
        P(("shard", "rep"), None),
        P(None, ("shard", "rep")),
        P(("shard", "rep")),
    )
    body = make_body(mesh.shape["shard"], mesh.shape["rep"])

    return jax.shard_map(
        body,
        mesh=mesh,
        in_specs=(rows, rows, P("rep", None)) + params * 3,
        out_specs=(rows, rows) + params * 4,
        check_vma=False,
    )
```

```python
import itertools
import math

import jax
import jax.numpy as jnp
from jax import lax
from jax.experimental import pallas as pl
from jax.experimental.pallas import tpu as pltpu
from jax.sharding import PartitionSpec as P


HEAD_DIM = 64


lr_rate = 0.03
beta_one = 0.9
beta_two = 0.95
adam_eps = 1e-08
weight_decay = 0.1
step_count = 3
norm_eps = 1e-05

f32 = jnp.float32
bf16 = jnp.bfloat16


def layer_norm(values_in):
    centred = values_in - jnp.mean(values_in, axis=-1, keepdims=True)
    inv_std = lax.rsqrt(jnp.mean(centred * centred, axis=-1, keepdims=True) + norm_eps)
    return (centred * inv_std, inv_std)


def norm_back(grad_normed, normed, inv_std):
    return inv_std * (
        grad_normed
        - jnp.mean(grad_normed, axis=-1, keepdims=True)
        - normed * jnp.mean(grad_normed * normed, axis=-1, keepdims=True)
    )


def adamw_step(weight, first_mom, second_mom, gradient):
    momentum = beta_one * first_mom + (1.0 - beta_one) * gradient
    variance = beta_two * second_mom + (1.0 - beta_two) * gradient * gradient
    fixed_mom = momentum / (1.0 - beta_one**step_count)
    fixed_var = variance / (1.0 - beta_two**step_count)
    return (
        weight - lr_rate * (fixed_mom / (jnp.sqrt(fixed_var) + adam_eps) + weight_decay * weight),
        momentum,
        variance,
    )


def dot_on(left_side, right_side, left_dim, right_dim):
    return lax.dot_general(
        left_side,
        right_side,
        (((left_dim,), (right_dim,)), ((), ())),
        preferred_element_type=f32,
    )


def dot_plain(left_side, right_side):
    return dot_on(left_side, right_side, 1, 0)


def dot_rows(left_side, right_side):
    return dot_on(left_side, right_side, 1, 1)


def dot_cols(left_side, right_side):
    return dot_on(left_side, right_side, 0, 0)


def masked_exp(query_head, key_head, same_doc):
    scores = dot_cols(key_head, query_head) * (1.0 / math.sqrt(HEAD_DIM))
    exp_scores = jnp.where(same_doc, jnp.exp(scores), 0.0)
    return exp_scores / jnp.sum(exp_scores, axis=0, keepdims=True)


def head_slices(head, heads, rows, stride, start):
    return [
        slice(base, base + rows)
        for base in range(head * stride + start, heads * stride * (HEAD_DIM // rows), heads * stride)
    ]


def read_head(ref, slices):
    return jnp.concatenate([ref[one, :] for one in slices], axis=0)


def write_head(ref, slices, value):
    rows = value.shape[0] // len(slices)
    for i, one in enumerate(slices):
        ref[one, :] = value[i * rows : (i + 1) * rows]


def fill(ref, pieces, start, stop):
    rows = stop - start
    for i, piece in enumerate(pieces):
        ref[i * rows : (i + 1) * rows, :] = piece[start:stop, :]


def split_out(far_ref, near_ref, make):
    half = near_ref.shape[0]
    far_ref[...] = make(slice(half, 2 * half)).astype(bf16)
    near_ref[...] = make(slice(0, half))


def attend_kernel(rows, in_rows, out_rows, unit_cols, count, *refs):
    pieces, refs = refs[:count], refs[count:]
    tokens, refs = refs[:-12], refs[-12:]
    picks_ref, seg_col_ref, seg_row_ref, *refs = refs
    w_in_ref, w_out_ref, group_ref, inner_ref, out_ref, coeff_ref, unit_ref, far_ref, near_ref = refs
    fill(w_in_ref, pieces, 0, in_rows)
    fill(w_out_ref, pieces, in_rows, in_rows + out_rows)
    fill(group_ref, tokens, 0, group_ref.shape[0] // len(tokens))
    small = [p[in_rows + out_rows :, :].astype(f32) for p in pieces]
    total = sum(small).astype(bf16)
    coeff_ref[...] = total
    unit_at = total.shape[0] // 2
    for i, one in enumerate(small):
        unit_ref[:, i * unit_cols : (i + 1) * unit_cols] = one[unit_at : unit_at + 1, :unit_cols]
    bias = dot_rows(picks_ref[...], total)
    product = dot_rows(w_in_ref[...], group_ref[...])
    heads = out_ref.shape[0] // HEAD_DIM
    blocks = HEAD_DIM // rows
    for slot in range(heads * blocks):
        base = slot * 3 * rows
        own = slice(slot * rows, (slot + 1) * rows)
        for i, add in enumerate((bias[own, 0:1], 0.0, bias[own, 1:2])):
            part = slice(base + i * rows, base + (i + 1) * rows)
            inner_ref[part, :] = (product[part] + add).astype(bf16)
    same_doc = seg_col_ref[...] == seg_row_ref[...]
    for head in range(heads):
        query, key, value = [
            read_head(inner_ref, head_slices(head, heads, rows, 3 * rows, i * rows))
            for i in range(3)
        ]
        probs = masked_exp(query, key, same_doc)
        attended = dot_plain(value, probs.astype(bf16)).astype(bf16)
        write_head(out_ref, head_slices(head, heads, rows, rows, 0), attended)
    split_out(far_ref, near_ref, lambda cols: dot_cols(out_ref[:, cols], w_out_ref[...]))


def units_kernel(start, stop, count, parts, *refs):
    pieces, refs = refs[:count], refs[count:]
    group, refs = refs[: -(parts + 4)], refs[-(parts + 4) :]
    unit_ref, w_ref, group_ref, slope_ref, *act_refs = refs
    fill(w_ref, pieces, start, stop)
    fill(group_ref, group, 0, group_ref.shape[0] // len(group))
    cols = act_refs[0].shape[1]
    for i, act_ref in enumerate(act_refs):
        own = slice(i * cols, (i + 1) * cols)
        hidden = dot_rows(group_ref[...], w_ref[own, :]) + unit_ref[:, own]
        bell = 0.5 * (1.0 + lax.erf(hidden * (1.0 / math.sqrt(2.0))))
        act_ref[...] = (hidden * bell).astype(bf16)
        slope = bell + hidden * jnp.exp(-0.5 * hidden * hidden) * (1.0 / math.sqrt(2.0 * math.pi))
        slope_ref[:, own] = slope


def shrink_kernel(count, *refs):
    pieces, refs = refs[:count], refs[count:]
    acts, (w_ref, far_ref, near_ref) = refs[:-3], refs[-3:]
    fill(w_ref, pieces, 0, pieces[0].shape[0])
    cols = acts[0].shape[1]

    def make(rows):
        terms = [
            dot_plain(act[rows, :], w_ref[i * cols : (i + 1) * cols, :])
            for i, act in enumerate(acts)
        ]
        return sum(terms[1:], terms[0])

    split_out(far_ref, near_ref, make)


def units_back_kernel(count, *refs):
    grads, refs = refs[:count], refs[count:]
    w_shrink_ref, w_expand_ref, slope_ref, group_ref, bias_ref, sum_ref, far_ref, near_ref = refs[:8]
    back_refs = refs[8:]
    fill(group_ref, grads, 0, grads[0].shape[0])
    cols = back_refs[0].shape[1]
    for i, back_ref in enumerate(back_refs):
        own = slice(i * cols, (i + 1) * cols)
        back = dot_rows(group_ref[...], w_shrink_ref[own, :]) * slope_ref[:, own]
        back_ref[...] = back.astype(bf16)
        sum_ref[:, own] = jnp.sum(back, axis=0, keepdims=True)

    def make(rows):
        terms = [
            dot_plain(back[rows, :], w_expand_ref[i * cols : (i + 1) * cols, :])
            for i, back in enumerate(back_refs)
        ]
        return sum(terms[1:], terms[0])

    split_out(far_ref, near_ref, make)
    bias_ref[...] = jnp.sum(group_ref[...].astype(f32), axis=0, keepdims=True)


def attend_back_kernel(rows, count, *refs):
    grads, refs = refs[:count], refs[count:]
    inner_ref, w_in_ref, w_out_ref, seg_col_ref, seg_row_ref = refs[:5]
    group_ref, shared_ref, out_ref, sum_ref, far_ref, near_ref, grad_ref = refs[5:]
    score_scale = 1.0 / math.sqrt(HEAD_DIM)
    own_rows = group_ref.shape[0] // count
    fill(group_ref, grads, 0, own_rows)
    grad_ref[...] = dot_rows(w_out_ref[...], group_ref[...]).astype(bf16)
    heads = grad_ref.shape[0] // HEAD_DIM
    same_doc = seg_col_ref[...] == seg_row_ref[...]
    for head in range(heads):
        slots = [head_slices(head, heads, rows, 3 * rows, i * rows) for i in range(3)]
        query, key, value = [read_head(inner_ref, one) for one in slots]
        outer = head_slices(head, heads, rows, rows, 0)
        grad = read_head(grad_ref, outer)
        probs = masked_exp(query, key, same_doc)
        prob_grad = dot_cols(value, grad)
        row_dots = jnp.sum(probs * prob_grad, axis=0, keepdims=True)
        score_half = (probs * (prob_grad - row_dots)).astype(bf16)
        dq = dot_plain(key, score_half) * score_scale
        dk = dot_rows(query, score_half) * score_scale
        dv = dot_rows(grad, probs.astype(bf16))
        for one, value_out in zip(slots, (dq, dk, dv)):
            write_head(out_ref, one, value_out.astype(bf16))
        for column, value_out in enumerate((dq, dv)):
            sums = jnp.sum(value_out, axis=1, keepdims=True)
            for i, one in enumerate(outer):
                sum_ref[one, column : column + 1] = sums[i * rows : (i + 1) * rows]
    split_out(far_ref, near_ref, lambda cols: dot_cols(out_ref[:, cols], w_in_ref[...]))
    bias = jnp.sum(group_ref[...].astype(f32), axis=0, keepdims=True)
    shared_ref[...] = sum(g[own_rows:, :].astype(f32) for g in grads)
    shared_ref[shared_ref.shape[0] - 1 :, :] = bias


def factor_rep(count, first):
    factors = [first]
    count //= first
    while count > 1:
        step = 4 if count % 4 == 0 else 2
        factors.append(step)
        count //= step
    return factors


def make_body(groups, replicas):
    shard_bits = [1 << i for i in range(groups.bit_length() - 1)]

    def swap(value, bit):
        return lax.ppermute(value, "shard", [(i, i ^ bit) for i in range(groups)])

    slot_order = sorted(range(groups), key=lambda i: (i & 1, i))

    def gather_group(piece):
        pieces = {0: piece}
        for bit in reversed(shard_bits):
            for slot in list(pieces):
                pieces[slot ^ bit] = swap(pieces[slot], bit)
        return [pieces[i] for i in slot_order]

    def scatter_group(near, far):
        total = near + swap(far, 1).astype(f32)
        for bit in reversed(shard_bits[1:]):
            half = total.shape[0] // 2
            came = swap(total[half:].astype(bf16), bit)
            total = total[:half] + came.astype(f32)
        return total

    def body(
        tokens,
        cotangent,
        segment_ids,
        intake,
        outlet,
        expand,
        shrink,
        affine,
        offset,
        intake_first,
        outlet_first,
        expand_first,
        shrink_first,
        affine_first,
        offset_first,
        intake_second,
        outlet_second,
        expand_second,
        shrink_second,
        affine_second,
        offset_second,
    ):
        own_rows = tokens.shape[1]
        width = tokens.shape[2]
        seq_len = own_rows * groups
        head_cols = intake.shape[1] * replicas
        factors = factor_rep(replicas, head_cols // HEAD_DIM)
        strides = [math.prod(factors[i + 1 :]) for i in range(len(factors))]
        lead = factors[0]
        suffixes = list(itertools.product(*[range(f) for f in factors[1:]]))
        own_shard = lax.axis_index("shard")
        own_rep = lax.axis_index("rep")

        bulk = len(factors) > 2
        aligned = intake.shape[1] % 16 == 0
        head_rows = intake.shape[1] if aligned else HEAD_DIM

        sent_as = {}

        def shift(value, level, amount, name):
            pairs = []
            for r in range(replicas):
                coord = (r // strides[level]) % factors[level]
                moved = (coord + amount) % factors[level]
                pairs.append((r, r + (moved - coord) * strides[level]))
            sent_as[name] = value
            return lax.ppermute(value, "rep", pairs)

        def gather_rep(piece, tag):
            parts = [piece] + [shift(piece, 0, k, f"{tag}_z{k}") for k in range(1, lead)]
            if bulk:
                return gather_rest({(): jnp.concatenate(parts, axis=0)})
            blocks = list(parts)
            for k in range(1, len(suffixes)):
                blocks += [shift(v, 1, k, f"{tag}_y{k}_{j}") for j, v in enumerate(parts)]
            return blocks

        def gather_rest(blocks):
            for level in range(1, len(factors)):
                joined = jnp.concatenate(list(blocks.values()), axis=0)
                grown = {s + (0,): v for s, v in blocks.items()}
                for k in range(1, factors[level]):
                    came = jnp.split(shift(joined, level, k, "bulk"), len(blocks))
                    grown.update({s + (k,): v for s, v in zip(blocks, came)})
                blocks = grown
            return [p for s in suffixes for p in jnp.split(blocks[s], lead)]

        def join(pieces, start, stop):
            return jnp.concatenate([p[start:stop] for p in pieces], axis=0)

        def order_heads(joined, kinds):
            split = joined.reshape(len(suffixes), lead, kinds, -1, joined.shape[1])
            return split.transpose(1, 2, 0, 3, 4).reshape(joined.shape)

        def by_suffix(left_side, right_side, kinds, parts):
            if aligned:
                count = len(suffixes) * parts
                rows = left_side.shape[0] // count
                products = [
                    dot_plain(left_side[i * rows : (i + 1) * rows], right_side)
                    for i in range(count)
                ]
                return [products[i * parts : (i + 1) * parts] for i in range(len(suffixes))]
            product = dot_plain(left_side, right_side)
            split = product.reshape(lead, kinds, len(suffixes), -1, product.shape[1])
            split = split.transpose(2, 0, 1, 3, 4)
            return [[p] for p in split.reshape(len(suffixes), -1, product.shape[1])]

        def wait_for(value, gate):
            return lax.optimization_barrier((value, *gate))[0] if gate else value

        def scatter_rep(blocks, tag, shared=None, units=None, gates=((), (), ())):
            if bulk:
                blocks = [[jnp.concatenate(parts, axis=0)] for parts in blocks]
            blocks = dict(zip(suffixes, blocks))
            units = {} if shared is None else dict(zip(suffixes, units))

            def pack(pieces, line):
                if line is None:
                    return jnp.concatenate([p.astype(bf16) for p in pieces], axis=0)
                line = jnp.pad(line, ((0, extra - small_rows - 1), (0, width - line.shape[1])))
                joined = [p.astype(bf16) for p in [*pieces, shared, line]]
                return jnp.concatenate(joined, axis=0)

            for level in reversed(range(1, len(factors))):
                merged = {s[:-1]: list(v) for s, v in blocks.items() if s[-1] == 0}
                lines = {s[:-1]: v for s, v in units.items() if s[-1] == 0}
                total = shared
                for k in range(1, factors[level]):
                    for part in reversed(range(len(next(iter(merged.values()))))):
                        line = None
                        if shared is not None and part == 0:
                            line = jnp.concatenate([units[s + (k,)] for s in merged], axis=1)
                        sent = pack([blocks[s + (k,)][part] for s in merged], line)
                        came = shift(sent, level, -k, f"{tag}_y{k}_{part}")
                        came = wait_for(came, gates[min(part, 1)]).astype(f32)
                        rows = blocks[next(iter(blocks))][part].shape[0]
                        for i, s in enumerate(merged):
                            merged[s][part] = merged[s][part] + came[i * rows : (i + 1) * rows]
                        if line is not None:
                            at = came.shape[0] - extra
                            total = total + came[at : at + small_rows]
                            size = line.shape[1] // len(merged)
                            row = came[at + small_rows][None]
                            for i, s in enumerate(merged):
                                lines[s] = lines[s] + row[:, i * size : (i + 1) * size]
                blocks, shared, units = merged, total, lines
            parts = blocks[()]
            per_part = lead // len(parts)
            rows = parts[0].shape[0] // per_part

            def slot(k):
                at = k % per_part * rows
                return parts[k // per_part][at : at + rows]

            result, total = slot(0), shared
            if shared is not None:
                size = units[()].shape[1] // lead
                line_total = units[()][:, :size]
            for k in range(1, lead):
                line = None if shared is None else units[()][:, k * size : (k + 1) * size]
                came = shift(pack([slot(k)], line), 0, -k, f"{tag}_z{k}")
                came = wait_for(came, gates[2]).astype(f32)
                result = result + came[:rows]
                if shared is not None:
                    total = total + came[rows : rows + small_rows]
                    line_total = line_total + came[rows + small_rows][None, :size]
            return result if shared is None else (result, total, line_total)

        extra = 16
        own_cols = affine.shape[1]
        own_start = (own_shard * replicas + own_rep) * own_cols
        small_rows = affine.shape[0]
        placed = lax.dynamic_update_slice(
            jnp.zeros((small_rows, width), bf16), affine.astype(bf16), (0, own_start)
        )
        unit_row = jnp.pad(
            offset.astype(bf16).reshape(1, -1),
            ((0, extra - small_rows - 1), (0, width - offset.shape[0])),
        )
        source = tokens.reshape(own_rows, width)
        own_small = jnp.pad(placed, ((0, extra - small_rows), (0, 0)))
        token_parts = gather_group(jnp.concatenate([source, own_small], axis=0))

        intake_low = intake.astype(bf16).reshape(-1, width)
        in_rows = intake_low.shape[0]
        out_rows = outlet.shape[0]
        wide_rows = expand.shape[0]
        pieces = gather_rep(
            jnp.concatenate([intake_low, outlet.astype(bf16), placed, unit_row], axis=0), "ga"
        )
        placed_group = sum(p[own_rows : own_rows + small_rows].astype(f32) for p in token_parts)
        placed_group = placed_group.astype(bf16)
        for level, factor in enumerate(factors):
            own_sum = placed_group
            for k in range(1, factor):
                placed_group = placed_group + shift(own_sum, level, k, f"gs_{level}_{k}")
        coeffs = placed_group.astype(f32)
        wide_pieces = gather_rep(expand.astype(bf16), "gb")
        shrink_pieces = gather_rep(shrink.astype(bf16), "gc")
        unit_cols = offset.shape[0]
        if not aligned:
            at = in_rows + out_rows
            line = jnp.concatenate([p[at + small_rows :][:1, :unit_cols] for p in pieces], axis=1)
            line = jnp.pad(line, ((0, extra - small_rows - 1), (0, width - line.shape[1])))
            placed_all = sum(p[at : at + small_rows].astype(f32) for p in pieces).astype(bf16)
            w_in = order_heads(join(pieces, 0, in_rows), 3)
            w_out = order_heads(join(pieces, in_rows, at), 1)
            pieces = [jnp.concatenate([w_in, w_out, placed_all, line], axis=0)]
            wide_pieces = [join(wide_pieces, 0, wide_rows)]
            shrink_pieces = [join(shrink_pieces, 0, wide_rows)]
            in_rows, out_rows = in_rows * replicas, out_rows * replicas
            wide_rows, unit_cols = wide_rows * replicas, unit_cols * replicas
        units = wide_rows * len(wide_pieces)

        index = lax.broadcasted_iota(jnp.int32, (head_cols, 1), 0)
        part_rows = intake.shape[1]
        if aligned:
            suffix_index = index // (lead * part_rows)
            lead_index = index // part_rows % lead
        else:
            lead_index = index // HEAD_DIM
            suffix_index = index // part_rows % len(suffixes)
        slot_index = lead_index * len(suffixes) + suffix_index
        feature_rep = jnp.zeros_like(index)
        for stride, factor in zip(strides, factors):
            slot_at = (slot_index // stride) % factor
            coord = (own_rep // stride) % factor
            feature_rep = feature_rep + ((coord - slot_at + factor) % factor) * stride
        feature = (own_shard * replicas + feature_rep) * own_cols + index % own_cols
        picks = feature == lax.broadcasted_iota(jnp.int32, (head_cols, width), 1)

        every_seg = segment_ids.reshape(seq_len)
        seg_slots = jnp.concatenate(
            [
                lax.dynamic_slice_in_dim(every_seg, (own_shard ^ k) * own_rows, own_rows)
                for k in slot_order
            ]
        )
        seg_col = seg_slots.reshape(seq_len, 1)
        seg_row = seg_slots.reshape(1, seq_len)

        def call(kernel, outs, *operands, scratch=()):
            return pl.pallas_call(
                kernel,
                out_shape=[jax.ShapeDtypeStruct(shape, dtype) for shape, dtype in outs],
                scratch_shapes=[pltpu.VMEM(shape, dtype) for shape, dtype in scratch],
            )(*operands)

        half = seq_len // 2
        full = (seq_len, width)
        two_halves = [((half, width), bf16), ((half, width), f32)]
        w_in, w_out, group_tokens, inner, attended, _, unit_bias, far, near = call(
            lambda *refs: attend_kernel(head_rows, in_rows, out_rows, unit_cols, len(pieces), *refs),
            [
                ((3 * head_cols, width), bf16),
                ((head_cols, width), bf16),
                (full, bf16),
                ((3 * head_cols, seq_len), bf16),
                ((head_cols, seq_len), bf16),
                ((extra, width), bf16),
                ((1, units), f32),
                *two_halves,
            ],
            *pieces,
            *token_parts,
            picks.astype(bf16),
            seg_col,
            seg_row,
        )
        attn_out = scatter_group(near, far)
        resid_one = source.astype(f32) + attn_out + coeffs[2]
        normed_one, inv_one = layer_norm(resid_one)
        mixed_one = normed_one * (1.0 + coeffs[3]) + coeffs[4]
        inner_parts = gather_group(mixed_one.astype(bf16))
        parts = 2
        count = parts * (1 if bulk else len(suffixes))
        thin = [((seq_len, units // count), bf16)] * count
        w_expand, group_in, slope, *acts = call(
            lambda *refs: units_kernel(0, wide_rows, len(wide_pieces), count, *refs),
            [((units, width), bf16), (full, bf16), ((seq_len, units), f32), *thin],
            *wide_pieces,
            *inner_parts,
            unit_bias,
        )
        w_shrink, far, near = call(
            lambda *refs: shrink_kernel(len(shrink_pieces), *refs),
            [((units, width), bf16), *two_halves],
            *shrink_pieces,
            *acts,
        )
        ffn_out = scatter_group(near, far)
        resid_two = mixed_one + ffn_out + coeffs[5]
        normed_two, inv_two = layer_norm(resid_two)
        layer_out = (normed_two * (1.0 + coeffs[6]) + coeffs[7]).astype(bf16)

        out_grad = cotangent.reshape(own_rows, width).astype(f32)
        grad_two = norm_back(out_grad * (1.0 + coeffs[6]), normed_two, inv_two)
        grad_parts = gather_group(grad_two.astype(bf16))
        gain_two = jnp.sum(out_grad * normed_two, axis=0)
        shift_two = jnp.sum(out_grad, axis=0)
        group_grad, bias_two, unit_sums, far, near, *backs = call(
            lambda *refs: units_back_kernel(groups, *refs),
            [(full, bf16), ((1, width), f32), ((1, units), f32), *two_halves, *thin],
            *grad_parts,
            w_shrink,
            w_expand,
            slope,
        )

        def unit_blocks(lefts, right_side):
            if bulk:
                product = dot_cols(jnp.concatenate(lefts, axis=1), right_side)
                return [[p] for p in jnp.split(product, len(suffixes))]
            products = [dot_cols(left, right_side) for left in lefts]
            return [products[i * parts : (i + 1) * parts] for i in range(len(suffixes))]

        grad_inner = scatter_group(near, far)
        grad_mixed = grad_two + grad_inner
        grad_one = norm_back(grad_mixed * (1.0 + coeffs[3]), normed_one, inv_one)
        gain_one = jnp.sum(grad_mixed * normed_one, axis=0)
        shift_one = jnp.sum(grad_mixed, axis=0)
        sums = jnp.stack([gain_one, shift_one, gain_two, shift_two])
        sums = jnp.pad(sums, ((0, extra - sums.shape[0]), (0, 0)))
        one_sent = jnp.concatenate([grad_one.astype(bf16), sums.astype(bf16)], axis=0)
        one_parts = gather_group(one_sent)
        group_one, sums, inner_grad, head_sums, far, near = call(
            lambda *refs: attend_back_kernel(head_rows, groups, *refs),
            [
                (full, bf16),
                ((extra, width), f32),
                (inner.shape, bf16),
                ((head_cols, 2), f32),
                *two_halves,
            ],
            *one_parts,
            inner,
            w_in,
            w_out,
            seg_col,
            seg_row,
            scratch=[((head_cols, seq_len), bf16)],
        )
        token_grad = (grad_one + scatter_group(near, far)).astype(bf16)
        bias_rows = lax.dot_general(
            head_sums,
            picks.astype(f32),
            (((0,), (0,)), ((), ())),
            precision=lax.Precision.HIGHEST,
            preferred_element_type=f32,
        )
        shared = jnp.concatenate(
            [bias_rows, sums[extra - 1 :], sums[0:2], bias_two, sums[2:4]], axis=0
        )
        intake_grad, affine_full, offset_grad = scatter_rep(
            by_suffix(inner_grad, group_tokens, 3, parts),
            "in",
            shared,
            jnp.split(unit_sums, len(suffixes), axis=1),
        )
        late = tuple(sent_as[f"in_z{k}"] for k in range(1, lead))
        last = (sent_as["in_y1_0"],)
        shrink_grad = scatter_rep(
            unit_blocks(acts, group_grad), "sh", gates=((one_sent,), (one_sent,), late)
        )
        expand_grad = scatter_rep(unit_blocks(backs, group_in), "ex", gates=(last, (far,), late))
        outlet_grad = scatter_rep(
            by_suffix(attended, group_one, 1, 1), "ou", gates=(last, last, late)
        )
        intake_grad = intake_grad.reshape(intake.shape)
        offset_grad = offset_grad.reshape(offset.shape)
        affine_grad = lax.dynamic_slice(affine_full, (0, own_start), affine.shape)

        intake_next, intake_momentum, intake_variance = adamw_step(
            intake, intake_first, intake_second, intake_grad
        )
        outlet_next, outlet_momentum, outlet_variance = adamw_step(
            outlet, outlet_first, outlet_second, outlet_grad
        )
        expand_next, expand_momentum, expand_variance = adamw_step(
            expand, expand_first, expand_second, expand_grad
        )
        shrink_next, shrink_momentum, shrink_variance = adamw_step(
            shrink, shrink_first, shrink_second, shrink_grad
        )
        affine_next, affine_momentum, affine_variance = adamw_step(
            affine, affine_first, affine_second, affine_grad
        )
        offset_next, offset_momentum, offset_variance = adamw_step(
            offset, offset_first, offset_second, offset_grad
        )
        return (
            layer_out.reshape(tokens.shape),
            token_grad.reshape(cotangent.shape),
            intake_grad,
            outlet_grad,
            expand_grad,
            shrink_grad,
            affine_grad,
            offset_grad,
            intake_next,
            outlet_next,
            expand_next,
            shrink_next,
            affine_next,
            offset_next,
            intake_momentum,
            outlet_momentum,
            expand_momentum,
            shrink_momentum,
            affine_momentum,
            offset_momentum,
            intake_variance,
            outlet_variance,
            expand_variance,
            shrink_variance,
            affine_variance,
            offset_variance,
        )

    return body


def solution(mesh):
    rows = P("rep", "shard", None)
    params = (
        P(None, ("shard", "rep"), None),
        P(("shard", "rep"), None),
        P(("shard", "rep"), None),
        P(("shard", "rep"), None),
        P(None, ("shard", "rep")),
        P(("shard", "rep")),
    )
    body = make_body(mesh.shape["shard"], mesh.shape["rep"])

    return jax.shard_map(
        body,
        mesh=mesh,
        in_specs=(rows, rows, P("rep", None)) + params * 3,
        out_specs=(rows, rows) + params * 4,
        check_vma=False,
    )
```

```python
import itertools
import math

import jax
import jax.numpy as jnp
from jax import lax
from jax.experimental import pallas as pl
from jax.experimental.pallas import tpu as pltpu
from jax.sharding import PartitionSpec as P


HEAD_DIM = 64


lr_rate = 0.03
beta_one = 0.9
beta_two = 0.95
adam_eps = 1e-08
weight_decay = 0.1
step_count = 3
norm_eps = 1e-05

f32 = jnp.float32
bf16 = jnp.bfloat16


def layer_norm(values_in):
    centred = values_in - jnp.mean(values_in, axis=-1, keepdims=True)
    inv_std = lax.rsqrt(jnp.mean(centred * centred, axis=-1, keepdims=True) + norm_eps)
    return (centred * inv_std, inv_std)


def norm_back(grad_normed, normed, inv_std):
    return inv_std * (
        grad_normed
        - jnp.mean(grad_normed, axis=-1, keepdims=True)
        - normed * jnp.mean(grad_normed * normed, axis=-1, keepdims=True)
    )


def adamw_step(weight, first_mom, second_mom, gradient):
    momentum = beta_one * first_mom + (1.0 - beta_one) * gradient
    variance = beta_two * second_mom + (1.0 - beta_two) * gradient * gradient
    fixed_mom = momentum / (1.0 - beta_one**step_count)
    fixed_var = variance / (1.0 - beta_two**step_count)
    return (
        weight - lr_rate * (fixed_mom / (jnp.sqrt(fixed_var) + adam_eps) + weight_decay * weight),
        momentum,
        variance,
    )


def dot_on(left_side, right_side, left_dim, right_dim):
    return lax.dot_general(
        left_side,
        right_side,
        (((left_dim,), (right_dim,)), ((), ())),
        preferred_element_type=f32,
    )


def dot_plain(left_side, right_side):
    return dot_on(left_side, right_side, 1, 0)


def dot_rows(left_side, right_side):
    return dot_on(left_side, right_side, 1, 1)


def dot_cols(left_side, right_side):
    return dot_on(left_side, right_side, 0, 0)


def masked_exp(query_head, key_head, same_doc):
    scores = dot_cols(key_head, query_head) * (1.0 / math.sqrt(HEAD_DIM))
    exp_scores = jnp.where(same_doc, jnp.exp(scores), 0.0)
    return exp_scores / jnp.sum(exp_scores, axis=0, keepdims=True)


def head_slices(head, heads, rows, stride, start):
    return [
        slice(base, base + rows)
        for base in range(head * stride + start, heads * stride * (HEAD_DIM // rows), heads * stride)
    ]


def read_head(ref, slices):
    return jnp.concatenate([ref[one, :] for one in slices], axis=0)


def write_head(ref, slices, value):
    rows = value.shape[0] // len(slices)
    for i, one in enumerate(slices):
        ref[one, :] = value[i * rows : (i + 1) * rows]


def fill(ref, pieces, start, stop):
    rows = stop - start
    for i, piece in enumerate(pieces):
        ref[i * rows : (i + 1) * rows, :] = piece[start:stop, :]


def split_out(far_ref, near_ref, make):
    half = near_ref.shape[0]
    far_ref[...] = make(slice(half, 2 * half)).astype(bf16)
    near_ref[...] = make(slice(0, half))


def attend_kernel(rows, in_rows, out_rows, unit_cols, count, *refs):
    pieces, refs = refs[:count], refs[count:]
    tokens, refs = refs[:-12], refs[-12:]
    picks_ref, seg_col_ref, seg_row_ref, *refs = refs
    w_in_ref, w_out_ref, group_ref, inner_ref, out_ref, coeff_ref, unit_ref, far_ref, near_ref = refs
    fill(w_in_ref, pieces, 0, in_rows)
    fill(w_out_ref, pieces, in_rows, in_rows + out_rows)
    fill(group_ref, tokens, 0, group_ref.shape[0] // len(tokens))
    small = [p[in_rows + out_rows :, :].astype(f32) for p in pieces]
    total = sum(small).astype(bf16)
    coeff_ref[...] = total
    unit_at = total.shape[0] // 2
    for i, one in enumerate(small):
        unit_ref[:, i * unit_cols : (i + 1) * unit_cols] = one[unit_at : unit_at + 1, :unit_cols]
    bias = dot_rows(picks_ref[...], total)
    product = dot_rows(w_in_ref[...], group_ref[...])
    heads = out_ref.shape[0] // HEAD_DIM
    blocks = HEAD_DIM // rows
    for slot in range(heads * blocks):
        base = slot * 3 * rows
        own = slice(slot * rows, (slot + 1) * rows)
        for i, add in enumerate((bias[own, 0:1], 0.0, bias[own, 1:2])):
            part = slice(base + i * rows, base + (i + 1) * rows)
            inner_ref[part, :] = (product[part] + add).astype(bf16)
    same_doc = seg_col_ref[...] == seg_row_ref[...]
    for head in range(heads):
        query, key, value = [
            read_head(inner_ref, head_slices(head, heads, rows, 3 * rows, i * rows))
            for i in range(3)
        ]
        probs = masked_exp(query, key, same_doc)
        attended = dot_plain(value, probs.astype(bf16)).astype(bf16)
        write_head(out_ref, head_slices(head, heads, rows, rows, 0), attended)
    split_out(far_ref, near_ref, lambda cols: dot_cols(out_ref[:, cols], w_out_ref[...]))


def units_kernel(start, stop, count, parts, *refs):
    pieces, refs = refs[:count], refs[count:]
    group, refs = refs[: -(parts + 4)], refs[-(parts + 4) :]
    unit_ref, w_ref, group_ref, slope_ref, *act_refs = refs
    fill(w_ref, pieces, start, stop)
    fill(group_ref, group, 0, group_ref.shape[0] // len(group))
    cols = act_refs[0].shape[1]
    for i, act_ref in enumerate(act_refs):
        own = slice(i * cols, (i + 1) * cols)
        hidden = dot_rows(group_ref[...], w_ref[own, :]) + unit_ref[:, own]
        bell = 0.5 * (1.0 + lax.erf(hidden * (1.0 / math.sqrt(2.0))))
        act_ref[...] = (hidden * bell).astype(bf16)
        slope = bell + hidden * jnp.exp(-0.5 * hidden * hidden) * (1.0 / math.sqrt(2.0 * math.pi))
        slope_ref[:, own] = slope


def shrink_kernel(count, *refs):
    pieces, refs = refs[:count], refs[count:]
    acts, (w_ref, far_ref, near_ref) = refs[:-3], refs[-3:]
    fill(w_ref, pieces, 0, pieces[0].shape[0])
    cols = acts[0].shape[1]

    def make(rows):
        terms = [
            dot_plain(act[rows, :], w_ref[i * cols : (i + 1) * cols, :])
            for i, act in enumerate(acts)
        ]
        return sum(terms[1:], terms[0])

    split_out(far_ref, near_ref, make)


def units_back_kernel(count, *refs):
    grads, refs = refs[:count], refs[count:]
    w_shrink_ref, w_expand_ref, slope_ref, group_ref, bias_ref, sum_ref, far_ref, near_ref = refs[:8]
    back_refs = refs[8:]
    fill(group_ref, grads, 0, grads[0].shape[0])
    cols = back_refs[0].shape[1]
    for i, back_ref in enumerate(back_refs):
        own = slice(i * cols, (i + 1) * cols)
        back = dot_rows(group_ref[...], w_shrink_ref[own, :]) * slope_ref[:, own]
        back_ref[...] = back.astype(bf16)
        sum_ref[:, own] = jnp.sum(back, axis=0, keepdims=True)

    def make(rows):
        terms = [
            dot_plain(back[rows, :], w_expand_ref[i * cols : (i + 1) * cols, :])
            for i, back in enumerate(back_refs)
        ]
        return sum(terms[1:], terms[0])

    split_out(far_ref, near_ref, make)
    bias_ref[...] = jnp.sum(group_ref[...].astype(f32), axis=0, keepdims=True)


def attend_back_kernel(rows, count, leads, parts, *refs):
    grads, refs = refs[:count], refs[count:]
    inner_ref, w_in_ref, w_out_ref, seg_col_ref, seg_row_ref, tokens_ref, outer_ref = refs[:7]
    group_ref, shared_ref, out_ref, sum_ref, far_ref, near_ref, *products, grad_ref = refs[7:]
    score_scale = 1.0 / math.sqrt(HEAD_DIM)
    own_rows = group_ref.shape[0] // count
    fill(group_ref, grads, 0, own_rows)
    grad_ref[...] = dot_rows(w_out_ref[...], group_ref[...]).astype(bf16)
    heads = grad_ref.shape[0] // HEAD_DIM
    same_doc = seg_col_ref[...] == seg_row_ref[...]
    for head in range(heads):
        slots = [head_slices(head, heads, rows, 3 * rows, i * rows) for i in range(3)]
        query, key, value = [read_head(inner_ref, one) for one in slots]
        outer = head_slices(head, heads, rows, rows, 0)
        grad = read_head(grad_ref, outer)
        probs = masked_exp(query, key, same_doc)
        prob_grad = dot_cols(value, grad)
        row_dots = jnp.sum(probs * prob_grad, axis=0, keepdims=True)
        score_half = (probs * (prob_grad - row_dots)).astype(bf16)
        dq = dot_plain(key, score_half) * score_scale
        dk = dot_rows(query, score_half) * score_scale
        dv = dot_rows(grad, probs.astype(bf16))
        for one, value_out in zip(slots, (dq, dk, dv)):
            write_head(out_ref, one, value_out.astype(bf16))
        for column, value_out in enumerate((dq, dv)):
            sums = jnp.sum(value_out, axis=1, keepdims=True)
            for i, one in enumerate(outer):
                sum_ref[one, column : column + 1] = sums[i * rows : (i + 1) * rows]
    split_out(far_ref, near_ref, lambda cols: dot_cols(out_ref[:, cols], w_in_ref[...]))
    bias = jnp.sum(group_ref[...].astype(f32), axis=0, keepdims=True)
    shared_ref[...] = sum(g[own_rows:, :].astype(f32) for g in grads)
    shared_ref[shared_ref.shape[0] - 1 :, :] = bias
    blocks = len(products) // parts
    for i in range(blocks):
        inner_products(
            (i, blocks),
            leads,
            ((out_ref, tokens_ref), (outer_ref, group_ref)),
            products[i * parts : (i + 1) * parts],
        )


def shrink_grad_kernel(count, *refs):
    acts, grads, outs = refs[:count], refs[count:-count], refs[-count:]
    group = jnp.concatenate([g[...] for g in grads], axis=0)
    for act, out in zip(acts, outs):
        out[...] = dot_cols(act[...], group).astype(out.dtype)


def inner_products(block, slots, pairs, outs):
    for part, out in enumerate(outs):
        products = []
        for left, right in pairs:
            rows = left.shape[0] // block[1] // len(outs)
            start = (block[0] * len(outs) + part) * rows
            products.append((dot_plain(left[start : start + rows, :], right[...]), rows // slots))
        at = 0
        for slot in range(slots):
            for product, rows in products:
                out[at : at + rows, :] = product[slot * rows : (slot + 1) * rows].astype(out.dtype)
                at += rows


def factor_rep(count, first):
    factors = [first]
    count //= first
    while count > 1:
        step = 4 if count % 4 == 0 else 2
        factors.append(step)
        count //= step
    return factors


def make_body(groups, replicas):
    shard_bits = [1 << i for i in range(groups.bit_length() - 1)]

    sent_as = {}

    def swap(value, bit, name):
        sent_as[name] = value
        return lax.ppermute(value, "shard", [(i, i ^ bit) for i in range(groups)])

    slot_order = sorted(range(groups), key=lambda i: (i & 1, i))

    def gather_group(piece, tag):
        pieces = {0: piece}
        for bit in reversed(shard_bits):
            for slot in list(pieces):
                pieces[slot ^ bit] = swap(pieces[slot], bit, f"{tag}_{bit}_{slot}")
        return [pieces[i] for i in slot_order]

    def scatter_group(near, far, tag):
        total = near + swap(far, 1, f"{tag}_1").astype(f32)
        for bit in reversed(shard_bits[1:]):
            half = total.shape[0] // 2
            came = swap(total[half:].astype(bf16), bit, f"{tag}_{bit}")
            total = total[:half] + came.astype(f32)
        return total

    def body(
        tokens,
        cotangent,
        segment_ids,
        intake,
        outlet,
        expand,
        shrink,
        affine,
        offset,
        intake_first,
        outlet_first,
        expand_first,
        shrink_first,
        affine_first,
        offset_first,
        intake_second,
        outlet_second,
        expand_second,
        shrink_second,
        affine_second,
        offset_second,
    ):
        own_rows = tokens.shape[1]
        width = tokens.shape[2]
        seq_len = own_rows * groups
        head_cols = intake.shape[1] * replicas
        factors = factor_rep(replicas, head_cols // HEAD_DIM)
        strides = [math.prod(factors[i + 1 :]) for i in range(len(factors))]
        lead = factors[0]
        suffixes = list(itertools.product(*[range(f) for f in factors[1:]]))
        own_shard = lax.axis_index("shard")
        own_rep = lax.axis_index("rep")

        bulk = len(factors) > 2
        aligned = intake.shape[1] % 16 == 0
        head_rows = intake.shape[1] if aligned else HEAD_DIM

        def shift(value, level, amount, name):
            pairs = []
            for r in range(replicas):
                coord = (r // strides[level]) % factors[level]
                moved = (coord + amount) % factors[level]
                pairs.append((r, r + (moved - coord) * strides[level]))
            sent_as[name] = value
            return lax.ppermute(value, "rep", pairs)

        def wait_for(value, gate):
            return lax.optimization_barrier((value, *gate))[0] if gate else value

        def gather_rep(piece, tag):
            parts = [piece] + [shift(piece, 0, k, f"{tag}_z{k}") for k in range(1, lead)]
            if bulk:
                return gather_rest({(): jnp.concatenate(parts, axis=0)})
            blocks = list(parts)
            for k in range(1, len(suffixes)):
                blocks += [shift(v, 1, k, f"{tag}_y{k}_{j}") for j, v in enumerate(parts)]
            return blocks

        def gather_rest(blocks):
            for level in range(1, len(factors)):
                joined = jnp.concatenate(list(blocks.values()), axis=0)
                grown = {s + (0,): v for s, v in blocks.items()}
                for k in range(1, factors[level]):
                    came = jnp.split(shift(joined, level, k, "bulk"), len(blocks))
                    grown.update({s + (k,): v for s, v in zip(blocks, came)})
                blocks = grown
            return [p for s in suffixes for p in jnp.split(blocks[s], lead)]

        def join(pieces, start, stop):
            return jnp.concatenate([p[start:stop] for p in pieces], axis=0)

        def order_heads(joined, kinds):
            split = joined.reshape(len(suffixes), lead, kinds, -1, joined.shape[1])
            return split.transpose(1, 2, 0, 3, 4).reshape(joined.shape)

        def by_suffix(left_side, right_side, kinds, parts):
            if aligned:
                count = len(suffixes) * parts
                rows = left_side.shape[0] // count
                products = [
                    dot_plain(left_side[i * rows : (i + 1) * rows], right_side)
                    for i in range(count)
                ]
                return [products[i * parts : (i + 1) * parts] for i in range(len(suffixes))]
            product = dot_plain(left_side, right_side)
            split = product.reshape(lead, kinds, len(suffixes), -1, product.shape[1])
            split = split.transpose(2, 0, 1, 3, 4)
            return [[p] for p in split.reshape(len(suffixes), -1, product.shape[1])]

        def scatter_rep(blocks, tag, shared=None, units=None, gates=((), ())):
            if bulk:
                blocks = [[jnp.concatenate(parts, axis=0)] for parts in blocks]
            blocks = dict(zip(suffixes, blocks))
            units = {} if shared is None else dict(zip(suffixes, units))

            def pack(pieces, line):
                if line is None:
                    return jnp.concatenate([p.astype(bf16) for p in pieces], axis=0)
                line = jnp.pad(line, ((0, extra - small_rows - 1), (0, width - line.shape[1])))
                joined = [p.astype(bf16) for p in [*pieces, shared, line]]
                return jnp.concatenate(joined, axis=0)

            for level in reversed(range(1, len(factors))):
                merged = {s[:-1]: list(v) for s, v in blocks.items() if s[-1] == 0}
                lines = {s[:-1]: v for s, v in units.items() if s[-1] == 0}
                total = shared
                for k in range(1, factors[level]):
                    if shared is not None:
                        line = jnp.concatenate([units[s + (k,)] for s in merged], axis=1)
                        came = shift(pack([], line), level, -k, f"{tag}_s{k}").astype(f32)
                        total = total + came[:small_rows]
                        size = line.shape[1] // len(merged)
                        row = came[small_rows][None]
                        for i, s in enumerate(merged):
                            lines[s] = lines[s] + row[:, i * size : (i + 1) * size]
                    for part in reversed(range(len(next(iter(merged.values()))))):
                        sent = pack([blocks[s + (k,)][part] for s in merged], None)
                        came = shift(sent, level, -k, f"{tag}_y{k}_{part}")
                        came = wait_for(came, gates[min(part, 1)]).astype(f32)
                        rows = blocks[next(iter(blocks))][part].shape[0]
                        for i, s in enumerate(merged):
                            merged[s][part] = merged[s][part] + came[i * rows : (i + 1) * rows]
                blocks, shared, units = merged, total, lines
            parts = blocks[()]
            per_part = lead // len(parts)
            rows = parts[0].shape[0] // per_part

            def slot(k):
                at = k % per_part * rows
                return parts[k // per_part][at : at + rows]

            size = 0 if shared is None else units[()].shape[1] // lead
            arrived = []
            for k in range(1, lead):
                line = None if shared is None else units[()][:, k * size : (k + 1) * size]
                arrived.append(shift(pack([slot(k)], line), 0, -k, f"{tag}_z{k}"))

            def finish(gate=()):
                result, total = slot(0), shared
                line_total = None if shared is None else units[()][:, :size]
                for came in arrived:
                    came = wait_for(came, gate).astype(f32)
                    result = result + came[:rows]
                    if shared is not None:
                        total = total + came[rows : rows + small_rows]
                        line_total = line_total + came[rows + small_rows][None, :size]
                return result if shared is None else (result, total, line_total)

            return finish

        extra = 16
        own_cols = affine.shape[1]
        own_start = (own_shard * replicas + own_rep) * own_cols
        small_rows = affine.shape[0]
        placed = lax.dynamic_update_slice(
            jnp.zeros((small_rows, width), bf16), affine.astype(bf16), (0, own_start)
        )
        unit_row = jnp.pad(
            offset.astype(bf16).reshape(1, -1),
            ((0, extra - small_rows - 1), (0, width - offset.shape[0])),
        )
        source = tokens.reshape(own_rows, width)
        own_small = jnp.pad(placed, ((0, extra - small_rows), (0, 0)))
        token_parts = gather_group(jnp.concatenate([source, own_small], axis=0), "tok")

        intake_low = intake.astype(bf16).reshape(-1, width)
        in_rows = intake_low.shape[0]
        out_rows = outlet.shape[0]
        wide_rows = expand.shape[0]
        pieces = gather_rep(
            jnp.concatenate([intake_low, outlet.astype(bf16), placed, unit_row], axis=0), "ga"
        )
        placed_group = sum(p[own_rows : own_rows + small_rows].astype(f32) for p in token_parts)
        placed_group = placed_group.astype(bf16)
        for level, factor in enumerate(factors):
            own_sum = placed_group
            for k in range(1, factor):
                placed_group = placed_group + shift(own_sum, level, k, f"gs_{level}_{k}")
        coeffs = placed_group.astype(f32)
        first_sent = (sent_as["ga_z1"],)
        wide_pieces = gather_rep(wait_for(expand, first_sent).astype(bf16), "gb")
        shrink_pieces = gather_rep(wait_for(shrink, first_sent).astype(bf16), "gc")
        unit_cols = offset.shape[0]
        if not aligned:
            at = in_rows + out_rows
            line = jnp.concatenate([p[at + small_rows :][:1, :unit_cols] for p in pieces], axis=1)
            line = jnp.pad(line, ((0, extra - small_rows - 1), (0, width - line.shape[1])))
            placed_all = sum(p[at : at + small_rows].astype(f32) for p in pieces).astype(bf16)
            w_in = order_heads(join(pieces, 0, in_rows), 3)
            w_out = order_heads(join(pieces, in_rows, at), 1)
            pieces = [jnp.concatenate([w_in, w_out, placed_all, line], axis=0)]
            wide_pieces = [join(wide_pieces, 0, wide_rows)]
            shrink_pieces = [join(shrink_pieces, 0, wide_rows)]
            in_rows, out_rows = in_rows * replicas, out_rows * replicas
            wide_rows, unit_cols = wide_rows * replicas, unit_cols * replicas
        units = wide_rows * len(wide_pieces)

        index = lax.broadcasted_iota(jnp.int32, (head_cols, 1), 0)
        part_rows = intake.shape[1]
        if aligned:
            suffix_index = index // (lead * part_rows)
            lead_index = index // part_rows % lead
        else:
            lead_index = index // HEAD_DIM
            suffix_index = index // part_rows % len(suffixes)
        slot_index = lead_index * len(suffixes) + suffix_index
        feature_rep = jnp.zeros_like(index)
        for stride, factor in zip(strides, factors):
            slot_at = (slot_index // stride) % factor
            coord = (own_rep // stride) % factor
            feature_rep = feature_rep + ((coord - slot_at + factor) % factor) * stride
        feature = (own_shard * replicas + feature_rep) * own_cols + index % own_cols
        picks = feature == lax.broadcasted_iota(jnp.int32, (head_cols, width), 1)

        every_seg = segment_ids.reshape(seq_len)
        seg_slots = jnp.concatenate(
            [
                lax.dynamic_slice_in_dim(every_seg, (own_shard ^ k) * own_rows, own_rows)
                for k in slot_order
            ]
        )
        seg_col = seg_slots.reshape(seq_len, 1)
        seg_row = seg_slots.reshape(1, seq_len)

        def call(kernel, outs, *operands, scratch=()):
            return pl.pallas_call(
                kernel,
                out_shape=[jax.ShapeDtypeStruct(shape, dtype) for shape, dtype in outs],
                scratch_shapes=[pltpu.VMEM(shape, dtype) for shape, dtype in scratch],
            )(*operands)

        half = seq_len // 2
        full = (seq_len, width)
        two_halves = [((half, width), bf16), ((half, width), f32)]
        w_in, w_out, group_tokens, inner, attended, _, unit_bias, far, near = call(
            lambda *refs: attend_kernel(head_rows, in_rows, out_rows, unit_cols, len(pieces), *refs),
            [
                ((3 * head_cols, width), bf16),
                ((head_cols, width), bf16),
                (full, bf16),
                ((3 * head_cols, seq_len), bf16),
                ((head_cols, seq_len), bf16),
                ((extra, width), bf16),
                ((1, units), f32),
                *two_halves,
            ],
            *pieces,
            *token_parts,
            picks.astype(bf16),
            seg_col,
            seg_row,
        )
        attn_out = scatter_group(near, far, "at")
        resid_one = source.astype(f32) + attn_out + coeffs[2]
        normed_one, inv_one = layer_norm(resid_one)
        mixed_one = normed_one * (1.0 + coeffs[3]) + coeffs[4]
        inner_parts = gather_group(mixed_one.astype(bf16), "x1")
        parts = 2
        count = parts * (1 if bulk else len(suffixes))
        thin = [((seq_len, units // count), bf16)] * count
        w_expand, group_in, slope, *acts = call(
            lambda *refs: units_kernel(0, wide_rows, len(wide_pieces), count, *refs),
            [((units, width), bf16), (full, bf16), ((seq_len, units), f32), *thin],
            *wide_pieces,
            *inner_parts,
            unit_bias,
        )
        w_shrink, far, near = call(
            lambda *refs: shrink_kernel(len(shrink_pieces), *refs),
            [((units, width), bf16), *two_halves],
            *shrink_pieces,
            *acts,
        )
        ffn_out = scatter_group(near, far, "ff")
        resid_two = mixed_one + ffn_out + coeffs[5]
        normed_two, inv_two = layer_norm(resid_two)
        layer_out = (normed_two * (1.0 + coeffs[6]) + coeffs[7]).astype(bf16)

        out_grad = cotangent.reshape(own_rows, width).astype(f32)
        grad_two = norm_back(out_grad * (1.0 + coeffs[6]), normed_two, inv_two)
        grad_parts = gather_group(grad_two.astype(bf16), "d2")
        gain_two = jnp.sum(out_grad * normed_two, axis=0)
        shift_two = jnp.sum(out_grad, axis=0)
        shrink_far = []
        if not bulk:
            shrink_far = call(
                lambda *refs: shrink_grad_kernel(count - parts, *refs),
                [((units // count, width), bf16)] * (count - parts),
                *acts[parts:],
                *grad_parts,
            )
        group_grad, bias_two, unit_sums, far, near, *backs = call(
            lambda *refs: units_back_kernel(groups, *refs),
            [(full, bf16), ((1, width), f32), ((1, units), f32), *two_halves, *thin],
            *grad_parts,
            w_shrink,
            w_expand,
            slope,
        )

        def unit_blocks(lefts, right_side, known=()):
            if bulk:
                product = dot_cols(jnp.concatenate(lefts, axis=1), right_side)
                return [[p] for p in jnp.split(product, len(suffixes))]
            products = [dot_cols(left, right_side) for left in lefts[: count - len(known)]]
            products += known
            return [products[i * parts : (i + 1) * parts] for i in range(len(suffixes))]

        grad_inner = scatter_group(near, far, "di")
        grad_mixed = grad_two + grad_inner
        grad_one = norm_back(grad_mixed * (1.0 + coeffs[3]), normed_one, inv_one)
        gain_one = jnp.sum(grad_mixed * normed_one, axis=0)
        shift_one = jnp.sum(grad_mixed, axis=0)
        sums = jnp.stack([gain_one, shift_one, gain_two, shift_two])
        sums = jnp.pad(sums, ((0, extra - sums.shape[0]), (0, 0)))
        one_sent = jnp.concatenate([grad_one.astype(bf16), sums.astype(bf16)], axis=0)
        one_parts = gather_group(one_sent, "o1")
        made = []
        if aligned:
            slot_rows = (in_rows + out_rows) * lead // parts
            for i in range(len(suffixes)):
                made += [((slot_rows, width), bf16 if i else f32)] * parts
        group_one, sums, inner_grad, head_sums, far, near, *made = call(
            lambda *refs: attend_back_kernel(head_rows, groups, lead // parts, parts, *refs),
            [
                (full, bf16),
                ((extra, width), f32),
                (inner.shape, bf16),
                ((head_cols, 2), f32),
                *two_halves,
                *made,
            ],
            *one_parts,
            inner,
            w_in,
            w_out,
            seg_col,
            seg_row,
            group_tokens,
            attended,
            scratch=[((head_cols, seq_len), bf16)],
        )
        token_grad = (grad_one + scatter_group(near, far, "tk")).astype(bf16)
        bias_rows = lax.dot_general(
            head_sums,
            picks.astype(f32),
            (((0,), (0,)), ((), ())),
            precision=lax.Precision.HIGHEST,
            preferred_element_type=f32,
        )
        shared = jnp.concatenate(
            [bias_rows, sums[extra - 1 :], sums[0:2], bias_two, sums[2:4]], axis=0
        )
        if aligned:
            inner_blocks = [made[i * parts : (i + 1) * parts] for i in range(len(suffixes))]
        else:
            inner_blocks = []
            for one, two in zip(
                by_suffix(inner_grad, group_tokens, 3, 1), by_suffix(attended, group_one, 1, 1)
            ):
                pair = [p[0].reshape(lead, -1, width) for p in (one, two)]
                inner_blocks.append([jnp.concatenate(pair, axis=1).reshape(-1, width)])
        shrink_done = scatter_rep(
            unit_blocks(acts, group_grad, shrink_far),
            "sh",
            gates=((one_sent,), (sent_as["di_2"],)),
        )
        expand_done = scatter_rep(
            unit_blocks(backs, group_in), "ex", gates=((far,), (sent_as["o1_1_2"],))
        )
        before = tuple(sent_as[f"ex_z{k}"] for k in range(1, lead))
        inner_done = scatter_rep(
            inner_blocks,
            "in",
            shared,
            jnp.split(unit_sums, len(suffixes), axis=1),
            gates=(before, before),
        )
        late = tuple(sent_as[f"in_z{k}"] for k in range(1, lead))
        shrink_grad = shrink_done(late)
        expand_grad = expand_done(late)
        joint_grad, affine_full, offset_grad = inner_done()
        intake_grad = joint_grad[: intake.shape[0] * intake.shape[1]].reshape(intake.shape)
        outlet_grad = joint_grad[intake.shape[0] * intake.shape[1] :]
        offset_grad = offset_grad.reshape(offset.shape)
        affine_grad = lax.dynamic_slice(affine_full, (0, own_start), affine.shape)

        intake_next, intake_momentum, intake_variance = adamw_step(
            intake, intake_first, intake_second, intake_grad
        )
        outlet_next, outlet_momentum, outlet_variance = adamw_step(
            outlet, outlet_first, outlet_second, outlet_grad
        )
        expand_next, expand_momentum, expand_variance = adamw_step(
            expand, expand_first, expand_second, expand_grad
        )
        shrink_next, shrink_momentum, shrink_variance = adamw_step(
            shrink, shrink_first, shrink_second, shrink_grad
        )
        affine_next, affine_momentum, affine_variance = adamw_step(
            affine, affine_first, affine_second, affine_grad
        )
        offset_next, offset_momentum, offset_variance = adamw_step(
            offset, offset_first, offset_second, offset_grad
        )
        return (
            layer_out.reshape(tokens.shape),
            token_grad.reshape(cotangent.shape),
            intake_grad,
            outlet_grad,
            expand_grad,
            shrink_grad,
            affine_grad,
            offset_grad,
            intake_next,
            outlet_next,
            expand_next,
            shrink_next,
            affine_next,
            offset_next,
            intake_momentum,
            outlet_momentum,
            expand_momentum,
            shrink_momentum,
            affine_momentum,
            offset_momentum,
            intake_variance,
            outlet_variance,
            expand_variance,
            shrink_variance,
            affine_variance,
            offset_variance,
        )

    return body


def solution(mesh):
    rows = P("rep", "shard", None)
    params = (
        P(None, ("shard", "rep"), None),
        P(("shard", "rep"), None),
        P(("shard", "rep"), None),
        P(("shard", "rep"), None),
        P(None, ("shard", "rep")),
        P(("shard", "rep")),
    )
    body = make_body(mesh.shape["shard"], mesh.shape["rep"])

    return jax.shard_map(
        body,
        mesh=mesh,
        in_specs=(rows, rows, P("rep", None)) + params * 3,
        out_specs=(rows, rows) + params * 4,
        check_vma=False,
    )
```
